512 devices in a mesh: tile: 32 (over z, core), chan: 16 (over y, x).
Axes of the slice: x: 4, y: 4, z: 16, core: 2. Of those that a mesh axis runs over, the one named last changes fastest.
Arguments:
- fields: float32 [64, 1024, 411], P('chan', 'tile'), may hold values from -12 to 12
- diffusivity: float32 [64, 1024], P('chan', 'tile'), may hold values from 0.02 to 0.24
- owners: int32 [4096, 1], replicated, may hold values from 0 to 31; in each aligned block of 128 rows (0 to 127, 128 to 255, ...) at most 8 rows name the same one
- observed: bfloat16 [8192, 6144], P('tile', 'chan'), may hold values from -6 to 6
- usable: int32 [8192], P('tile'), may hold values 0 or 1
- w_hidden: bfloat16 [411, 2048], P(None, 'chan'), may hold values from -0.3125 to 0.3125
- b_hidden: float32 [2048], P('chan'), may hold values from -3 to 3
- w_radiance: bfloat16 [2048, 6144], P(None, 'chan'), may hold values from -0.125 to 0.125
- b_radiance: float32 [6144], P('chan'), may hold values from -3 to 3
- inv_cov: bfloat16 [6144, 6144], P('tile', 'chan'), may hold values from -6 to 22
Outputs:
- gradient: float32 [64, 1024, 411], P('chan', 'tile')
The draws below stay inside these ranges and needn't reach their ends.
Inputs may be any that keep to these rules, and one draw needn't show every extreme that they name: `owners`: in each tile's block of 128 consecutive entries no owner appears more than 8 times, and in some blocks one appears exactly 8 times.
All inputs are finite; a program needn't handle non-finite values. No bound on the sum of `usable` on one device may be relied on, other than what follows from the above.
Results may differ from the reference program's by a relative error of at most 0.0045.
Values may be sent and summed in bfloat16 or wider, within the bound.
A program may use at most 64 MiB of HBM per device.

```python
import math
import jax
import jax.numpy as jnp
import numpy as np
from jax import lax

FEAT = 411
HID = 2048
NCH = 6144
NX = 64
NY = 1024
SRC_COLS = 8
COLS = 4096
CAPACITY = 8
SLOTS = 256
PROFILES = 8192
N_TILE = 32
N_CHAN = 16


def draw_inv_cov(key, part):
    first, second = jax.random.split(key)
    entries = jax.random.truncated_normal(first, -4.0, 4.0, (NCH, NCH), jnp.float32)
    coupling = (entries + entries.T) * (0.45 / math.sqrt(2.0 * NCH))
    scales = jnp.exp(jax.random.uniform(second, (NCH,), jnp.float32, 0.0, math.log(16.0)) * 0.5)
    matrix = scales[:, None] * (jnp.eye(NCH, dtype=jnp.float32) + coupling) * scales[None, :]
    return matrix.astype(jnp.bfloat16)


def place_ends(values, own_key, low, largest):
    extent = values.shape
    index_at = [jax.random.randint(jax.random.fold_in(own_key, axis), (), 0, extent[axis]) for axis in range(len(extent))]
    values = values.at[tuple(index_at)].set(low)
    longest = extent.index(max(extent))
    index_at[longest] = (index_at[longest] + 1) % extent[longest]
    return values.at[tuple(index_at)].set(largest)


def levels(stream_key, shape, shards, smallest, high):
    loudness, own = 1.0, jax.random.fold_in(stream_key, 6)
    for position, shards_of in shards:
        steps = jnp.exp(jax.random.uniform(jax.random.fold_in(own, position), (shards_of,), jnp.float32, smallest / len(shards), high / len(shards)))
        loudness = loudness * jnp.repeat(steps, shape[position] // shards_of).reshape([-1 if axis == position else 1 for axis in range(len(shape))])
    return loudness


def assign_block(rng, own, number, rows, number_of, top, limit, slope):
    sequence = jax.random.permutation(rng, number_of)
    crowded, common = portions_of(number_of, rows * top, limit, slope, True), portions_of(number_of, rows * top, limit, slope, False)
    places = jnp.arange(number_of)

    def named(lengths, rotation):
        used = int((lengths > 0).sum())
        fixed = max(1, used // 4)
        passed = fixed + (places - fixed + rotation * (used - fixed)) % max(1, number_of - fixed)
        return jnp.zeros((number_of,), jnp.int32).at[sequence[jnp.where(places < fixed, places, passed)]].set(jnp.asarray(lengths, jnp.int32))

    lengths = jnp.where(number % 4 == 0, named(crowded, number // 4), named(common, number - number // 4 - 1))
    mixed = jax.random.permutation(jax.random.fold_in(own, 3), number_of)
    source_of, sink = mixed[0:number_of // 2 * 2:2], mixed[1:number_of // 2 * 2:2]
    room = jnp.minimum(lengths[source_of] - 1, limit - lengths[sink]) // 2
    room = jnp.where((source_of == sequence[0]) | (sink == sequence[0]) | (lengths[sink] == 0), 0, jnp.maximum(room, 0))
    passed = jax.random.randint(jax.random.fold_in(own, 4), (number_of // 2,), 0, 1 << 20) % (room + 1)
    lengths = lengths.at[source_of].add(-passed).at[sink].add(passed)
    items = jnp.searchsorted(jnp.cumsum(lengths), jnp.arange(rows * top), side="right").astype(jnp.int32)
    listing = items.reshape(top, rows).T
    listing = listing[jax.random.permutation(jax.random.fold_in(own, 1), rows)]
    rotation = jax.random.randint(jax.random.fold_in(own, 2), (rows, 1), 0, top)
    return jnp.take_along_axis(listing, (jnp.arange(top)[None, :] + rotation) % top, axis=1)


def portions_of(number_of, total, reach, lean, full):
    loads = [(1 << 20) // math.isqrt(grade ** lean) + 1 for grade in range(1, number_of + 1)]
    largest = reach if full else min(reach, max(-(-total // number_of), total * loads[0] // sum(loads)))
    least = 1 if total - largest >= number_of - 1 else 0
    given, surplus = [largest] + [least] * (number_of - 1), total - largest - least * (number_of - 1)
    while surplus > 0:
        free = [i for i in range(1, number_of) if given[i] < largest] or [i for i in range(1, number_of) if given[i] < reach]
        whole, budget = sum([loads[i] for i in free]), surplus
        for i in free:
            more = min(reach - given[i], max(1, budget * loads[i] // whole), surplus)
            given[i] = given[i] + more
            surplus = surplus - more
    return np.array(given)


def gaussian(stream_key, extent, scale, bound, cuts=(), kind=jnp.bfloat16):
    values = scale * jax.random.normal(stream_key, extent, jnp.float32)
    if cuts:
        values = values * levels(stream_key, extent, cuts, -0.22, 0.18)
    return jnp.clip(values, -bound, bound).astype(kind)


def setup_inputs(seed: int = 0) -> dict:
    seeds = jax.random.split(jax.random.key(seed), 11)
    fields = gaussian(seeds[0], (NX, NY, FEAT), 2.0, 12.0, ((0, 16), (1, 32)), jnp.float32)
    diffusivity = jnp.clip(jnp.exp(math.log(0.24) - 2.4849066 * jax.random.uniform(seeds[1], (NX, NY), jnp.float32) ** levels(seeds[1], (NX, NY), ((0, 16), (1, 32)), -0.2, 0.2)), 0.02, 0.24)
    owners_keys = jax.random.split(jax.random.fold_in(seeds[2], 1), COLS // (N_CHAN * SRC_COLS))
    owners_turns = jax.random.permutation(jax.random.fold_in(seeds[2], 3), COLS // (N_CHAN * SRC_COLS))
    owners = jax.vmap(lambda own, number: assign_block(jax.random.fold_in(seeds[2], 2), own, number, N_CHAN * SRC_COLS, N_TILE, 1, CAPACITY, 2))(owners_keys, owners_turns).reshape((COLS, 1))
    observed = gaussian(seeds[3], (PROFILES, NCH), 1.0, 6.0, ((0, 32), (1, 16)))
    usable = place_ends((jax.random.randint(seeds[4], (PROFILES,), 0, 4) < 3).astype(jnp.int32), jax.random.fold_in(seeds[4], 1), 0, 1)
    w_hidden = gaussian(seeds[5], (FEAT, HID), FEAT ** -0.5, 0.3125, ((1, 16),))
    b_hidden = gaussian(seeds[6], (HID,), 0.5, 3.0, ((0, 16),), jnp.float32)
    w_radiance = gaussian(seeds[7], (HID, NCH), HID ** -0.5, 0.125, ((1, 16),))
    b_radiance = gaussian(seeds[8], (NCH,), 0.5, 3.0, ((0, 16),), jnp.float32)
    inv_cov = draw_inv_cov(jax.random.fold_in(seeds[10], 71), 0)
    return {"fields": fields, "diffusivity": diffusivity, "owners": owners, "observed": observed, "usable": usable, "w_hidden": w_hidden, "b_hidden": b_hidden, "w_radiance": w_radiance, "b_radiance": b_radiance, "inv_cov": inv_cov}


def diffuse(adjoint, kappa_root):
    root_pad = jnp.pad(kappa_root, ((1, 1), (0, 0)))
    coef_north = (kappa_root * root_pad[2:])[:, :, None]
    coef_south = (kappa_root * root_pad[:-2])[:, :, None]
    coef_east = (kappa_root * jnp.roll(kappa_root, -1, axis=1))[:, :, None]
    coef_west = (kappa_root * jnp.roll(kappa_root, 1, axis=1))[:, :, None]
    for sweep_index in range(2):
        padded = jnp.pad(adjoint, ((1, 1), (0, 0), (0, 0)))
        adjoint = adjoint + coef_north * (padded[2:] - adjoint) + coef_south * (padded[:-2] - adjoint) + coef_east * (jnp.roll(adjoint, -1, axis=1) - adjoint) + coef_west * (jnp.roll(adjoint, 1, axis=1) - adjoint)
    return adjoint

def reference(fields, diffusivity, owners, observed, usable, w_hidden, b_hidden, w_radiance, b_radiance, inv_cov):
    tile_cols = N_CHAN * SRC_COLS
    grouped = fields.reshape(N_CHAN, 4, N_TILE * SRC_COLS, 4, FEAT)
    averaged = lax.optimization_barrier(jnp.sum(grouped, axis=(1, 3))) * 0.0625
    ordered = averaged.reshape(N_CHAN, N_TILE, SRC_COLS, FEAT).transpose(1, 0, 2, 3).reshape(COLS, FEAT)
    ordered = ordered.astype(jnp.bfloat16)
    owner_table = owners[:, 0].reshape(N_TILE, tile_cols)
    owner_hits = (owner_table[:, :, None] == jnp.arange(N_TILE, dtype=jnp.int32)[None, None, :]).astype(jnp.int32)
    before = lax.optimization_barrier(jnp.sum((jnp.cumsum(owner_hits, axis=1) - owner_hits) * owner_hits, axis=2))
    tallies = lax.optimization_barrier(jnp.sum(owner_hits, axis=1))
    source_tile = jnp.arange(N_TILE, dtype=jnp.int32)[:, None]
    slot_index = (owner_table * SLOTS + source_tile * CAPACITY + before).reshape(COLS).astype(jnp.int32)
    stacked = jnp.zeros((PROFILES, FEAT), jnp.bfloat16).at[slot_index].set(ordered)
    occupied = (jnp.arange(CAPACITY, dtype=jnp.int32)[None, None, :] < tallies.T[:, :, None]).reshape(PROFILES)
    in_use = usable.astype(jnp.float32) * occupied.astype(jnp.float32)
    preact = jnp.dot(stacked, w_hidden, preferred_element_type=jnp.float32) + b_hidden[None, :]
    squash = jax.nn.sigmoid(preact)
    active = (preact * squash).astype(jnp.bfloat16)
    radiance = jnp.dot(active, w_radiance, preferred_element_type=jnp.float32) + b_radiance[None, :]
    departure = ((radiance - observed.astype(jnp.float32)) * in_use[:, None]).astype(jnp.bfloat16)
    cotangent = jnp.dot(departure, inv_cov, preferred_element_type=jnp.float32).astype(jnp.bfloat16)
    grad_hidden = jnp.dot(cotangent, w_radiance.T, preferred_element_type=jnp.float32)
    slope_term = squash * (1.0 + preact * (1.0 - squash))
    grad_pre = (grad_hidden * slope_term).astype(jnp.bfloat16)
    profile_grad = jnp.dot(grad_pre, w_hidden.T, preferred_element_type=jnp.float32)
    column_grad = profile_grad[slot_index]
    column_grad = column_grad.reshape(N_TILE, N_CHAN, SRC_COLS, FEAT).transpose(1, 0, 2, 3)
    column_grad = column_grad.reshape(N_CHAN, N_TILE * SRC_COLS, FEAT)
    spread = jnp.repeat(jnp.repeat(column_grad, 4, axis=0), 4, axis=1) * 0.0625
    return diffuse(spread, jnp.sqrt(diffusivity))
```

```python
import jax
import jax.numpy as jnp
from jax import lax
from jax.experimental import pallas as pl
from jax.experimental.pallas import tpu as pltpu
from jax.sharding import PartitionSpec as P

MESH = pl.DeviceIdType.MESH
F32, BF16 = jnp.float32, jnp.bfloat16
NZ, SIDE, NC, NT = 16, 4, 16, 32
CAP = 8
OWN = 8
TC = 128
FEAT, LANES = 411, 512
HID, ALL_HID = 128, 2048
CH = 384
ROWS = 192
HALF = ROWS // 2
UNUSED = 2.0**100

SEMS = (
    "ag1", "ag2", "diff", "obs", "r1a", "r1b", "r2a", "r2b", "core", "a1a", "a1b", "a2a", "a2b", "rs5", "halo",
)


def kernel(
    fields_h, diff_in, owners_in, obs_h, usable_in, wh_h, bh_in, wr_h, br_in, ic_h,
    out,
    fields, quads, obs_send, obs_recv, wh, wr, ic,
    cols, act, gp, r1a, r1b, s1a, s1b, r2a, r2b, g_all, dep, pgrad, rs5, halo, diff, strips, sweep,
    local, send, recv, ring_s, ring_r, hello,
):
    t, c = lax.axis_index("tile"), lax.axis_index("chan")
    z, k = t // 2, t % 2
    y, x = c // SIDE, c % SIDE
    sem_of = {name: i for i, name in enumerate(SEMS)}

    def tile_at(dz, core):
        return lax.rem(z + dz + NZ, NZ) * 2 + core

    def mod(v, n):
        return lax.rem(v + n, n)

    def push(src, dst, name, where):
        i = sem_of[name]
        pltpu.make_async_remote_copy(
            src_ref=src, dst_ref=dst, send_sem=send.at[i], recv_sem=recv.at[i],
            device_id=where, device_id_type=MESH,
        ).start()

    def wait_recv(ref, name):
        pltpu.make_async_copy(ref, ref, recv.at[sem_of[name]]).wait()

    def wait_send(ref, name):
        pltpu.make_async_copy(ref, ref, send.at[sem_of[name]]).wait()

    loads = [
        pltpu.make_async_copy(src, dst, local.at[i])
        for i, (src, dst) in enumerate(
            [(fields_h, fields), (ic_h, ic), (wr_h, wr), (obs_h, obs_send), (wh_h, wh)]
        )
    ]
    for copy in loads:
        copy.start()
    near = [(dz, core) for dz in (4, -4, 3, -3, 2, -2, 1, -1) for core in (0, 1)]
    around = [(dt, dc) for dt in (-1, 0, 1) for dc in (-1, 0, 1) if (dt, dc) != (0, 0)]
    barrier = pltpu.get_barrier_semaphore()
    greeted = [(t, mod(c + i, NC)) for i in range(1, NC)]
    greeted += [(tile_at(dz, core), c) for dz, core in near] + [(z * 2 + 1 - k, c)]
    greeted += [(mod(t + dt, NT), mod(c + dc, NC)) for dt, dc in around if dt and dc]
    for where in greeted:
        pl.semaphore_signal(barrier, inc=1, device_id=where, device_id_type=MESH)

    loads[0].wait()
    summed = fields[0] + fields[1] + fields[2] + fields[3]
    for b in range(LANES // 128):
        width = min(128, FEAT - b * 128)
        quads[b] = jnp.zeros((32, 128), F32)
        quads[b, :, 0:width] = summed[:, b * 128 : b * 128 + width]
        total = None
        for j in range(4):
            part = quads[b, pl.ds(j, OWN, stride=4), :]
            total = part if total is None else total + part
        cols[c, :, b * 128 : b * 128 + 128] = (total * 0.0625).astype(BF16)

    diff[4] = jnp.zeros((8, 128), F32)
    diff[4, 0:4, 0:32] = diff_in[...]

    own_row = jnp.broadcast_to(owners_in[pl.ds(t, 1), :].astype(F32), (TC, TC))
    own_col = jnp.transpose(own_row)
    at_row = lax.broadcasted_iota(jnp.int32, (TC, TC), 0)
    at_lane = lax.broadcasted_iota(jnp.int32, (TC, TC), 1)
    earlier = jnp.where((own_row == own_col) & (at_lane < at_row), 1.0, 0.0)
    rank = jnp.sum(earlier, axis=1, keepdims=True)
    slot = (own_col[:, 0:1] * float(CAP) + rank).astype(jnp.int32)
    select = jnp.where(
        slot == lax.broadcasted_iota(jnp.int32, (TC, NT * CAP), 1), 1.0, 0.0
    ).astype(BF16)

    loads[3].wait()
    usable = usable_in[...].astype(F32)
    usable = jnp.transpose(jnp.concatenate([usable] * 4, axis=0))
    for h in range(2):
        part = slice(h * 16, h * 16 + 16)
        seen = obs_send[part].astype(F32).reshape(TC, CH)
        seen = jnp.where(usable[:, h : h + 1] > 0.5, seen, UNUSED)
        obs_send[part] = seen.reshape(16, CAP, CH).astype(BF16)

    loads[1].wait()
    loads[2].wait()
    cov = ic[...]
    for b in range(NC // 2):
        part = lax.dot_general(
            cov, wr[b * 256 : b * 256 + 256, :], (((1,), (1,)), ((), ())), preferred_element_type=F32
        ).astype(BF16)
        for h in range(2):
            q = 2 * b + h
            gp[q // SIDE, q % SIDE] = part[:, h * 128 : h * 128 + 128]

    pl.semaphore_wait(barrier, len(greeted))

    for i in range(1, NC):
        push(cols.at[c], cols.at[c], "ag1", (t, mod(c + i, NC)))
    for i, (dt, dc) in enumerate(around):
        push(diff.at[4], diff.at[i if i < 4 else i + 1], "diff", (mod(t + dt, NT), mod(c + dc, NC)))
    for step in (SIDE, -SIDE):
        pl.semaphore_signal(hello, inc=1, device_id=(tile_at(step, k), c), device_id_type=MESH)
    own_obs = pltpu.make_async_copy(obs_send.at[t], obs_recv.at[t], local.at[5])
    own_obs.start()

    def send_obs(peers):
        for dz, core in peers:
            to = tile_at(dz, core)
            push(obs_send.at[to], obs_recv.at[t], "obs", (to, c))

    send_obs(near)
    send_obs([(0, 1 - k)])
    for d in range(1, SIDE):
        to_x, to_y = mod(x + d, SIDE), mod(y + d, SIDE)
        push(gp.at[:, to_x, 0:HALF, :], r1a.at[d - 1], "r1a", (t, y * SIDE + to_x))
        push(gp.at[to_y, :, HALF:ROWS, :], r1b.at[d - 1], "r1b", (t, to_y * SIDE + x))
    pl.semaphore_wait(hello, 2)
    send_obs([(dz, core) for dz in (8, 7, -7, 6, -6, 5, -5) for core in (0, 1)])

    loads[4].wait()
    wait_recv(cols.at[0 : NC - 1], "ag1")
    tile_cols = cols[...].astype(F32).reshape(TC, LANES)[:, 0:FEAT].astype(BF16)
    preact = jnp.dot(tile_cols, wh[...], preferred_element_type=F32) + bh_in[...]
    squash = jax.nn.sigmoid(preact)
    act[c] = (preact * squash).astype(BF16)
    slope = squash * (1.0 + preact * (1.0 - squash))
    for i in range(1, NC):
        push(act.at[c], act.at[c], "ag2", (t, mod(c + i, NC)))

    def add(own, got):
        acc = own.astype(F32)
        for d in range(SIDE - 1):
            acc = acc + got[d].astype(F32)
        return acc.astype(BF16)

    wait_recv(r1a, "r1a")
    s1a[...] = add(gp[:, x, 0:HALF, :], r1a)
    wait_recv(r1b, "r1b")
    s1b[...] = add(gp[y, :, HALF:ROWS, :], r1b)
    for d in range(1, SIDE):
        to_x, to_y = mod(x + d, SIDE), mod(y + d, SIDE)
        push(s1a.at[to_y], r2a.at[d - 1], "r2a", (t, to_y * SIDE + x))
        push(s1b.at[to_x], r2b.at[d - 1], "r2b", (t, y * SIDE + to_x))
    wait_recv(r2a, "r2a")
    g_all[z, k, 0:HALF, :] = add(s1a[y], r2a)
    wait_recv(r2b, "r2b")
    g_all[z, k, HALF:ROWS, :] = add(s1b[x], r2b)

    def ring_copy(s, way):
        block = g_all.at[mod(z - s * way, NZ), k]
        i = 0 if way == 1 else 1
        return pltpu.make_async_remote_copy(
            src_ref=block, dst_ref=block, send_sem=ring_s.at[i, s], recv_sem=ring_r.at[i, s],
            device_id=(tile_at(way, k), c), device_id_type=MESH,
        )

    ways = {1: NZ // 2, -1: NZ // 2 - 1}

    def to_core(zz):
        block = g_all.at[zz, k]
        push(block, block, "core", (z * 2 + 1 - k, c))

    def ring_step(s):
        for way, steps in ways.items():
            if 1 <= s <= steps:
                ring_copy(s - 1, way).wait_recv()
            if s < steps:
                ring_copy(s, way).start()
            if 1 <= s <= steps:
                to_core(mod(z - s * way, NZ))

    ring_step(0)
    to_core(z)

    wait_recv(act.at[0 : NC - 1], "ag2")
    tile_act = jnp.concatenate([act[i] for i in range(NC)], axis=1)
    radiance = jnp.dot(tile_act, wr[...], preferred_element_type=F32) + br_in[...]
    own_obs.wait()
    wait_recv(obs_recv.at[0 : NT - 1], "obs")
    arrived = obs_recv[...].astype(F32).reshape(NT * CAP, CH).astype(BF16)
    seen = jnp.dot(select, arrived, preferred_element_type=F32)
    dep[y, x] = jnp.where(seen < UNUSED * 0.5, radiance - seen, 0.0).astype(BF16)
    lo, hi = slice(0, TC // 2), slice(TC // 2, TC)
    for d in range(1, SIDE):
        to_x, to_y = mod(x + d, SIDE), mod(y + d, SIDE)
        push(dep.at[y, x, lo, :], dep.at[y, x, lo, :], "a1a", (t, y * SIDE + to_x))
        push(dep.at[y, x, hi, :], dep.at[y, x, hi, :], "a1b", (t, to_y * SIDE + x))
    ring_step(1)
    ring_step(2)
    wait_recv(dep.at[0, 0:3, lo, :], "a1a")
    for d in range(1, SIDE):
        push(dep.at[y, :, lo, :], dep.at[y, :, lo, :], "a2a", (t, mod(y + d, SIDE) * SIDE + x))
    wait_recv(dep.at[0, 0:3, hi, :], "a1b")
    for d in range(1, SIDE):
        push(dep.at[:, x, hi, :], dep.at[:, x, hi, :], "a2b", (t, y * SIDE + mod(x + d, SIDE)))
    for s in range(3, NZ // 2 + 1):
        ring_step(s)

    wait_recv(diff.at[0:8], "diff")
    lane = lax.broadcasted_iota(jnp.int32, (8, 128), 1)
    row = lax.broadcasted_iota(jnp.int32, (8, 128), 0)
    bands = []
    for dc in range(3):
        west, mid, east = (diff[8 - (dt * 3 + dc)] for dt in range(3))
        bands.append(
            jnp.where(
                lane < 8,
                pltpu.roll(west, 104, 1),
                jnp.where(lane < 40, pltpu.roll(mid, 8, 1), pltpu.roll(east, 40, 1)),
            )
        )
    upper = jnp.where(c > 0, pltpu.roll(bands[0], 6, 0), 0.0)
    lower = jnp.where(c < NC - 1, pltpu.roll(bands[2], 6, 0), 0.0)
    root = jnp.where(row < 2, upper, jnp.where(row < 6, pltpu.roll(bands[1], 2, 0), lower))
    root = jnp.sqrt(jnp.where((lane < 6) | (lane > 41), 0.0, root))
    root = jnp.transpose(root)[0:48, :]
    to_east = root * pltpu.roll(root, 47, 0)
    to_west = root * pltpu.roll(root, 1, 0)

    wait_recv(dep.at[0:3, :, lo, :], "a2a")
    wait_recv(dep.at[0:3, :, hi, :], "a2b")
    wait_recv(g_all.at[:, 0], "core")
    grad = jnp.zeros((TC, HID), F32)
    for b in range(NC):
        grad = grad + jnp.dot(
            dep[b // SIDE, b % SIDE], g_all[b].reshape(2 * ROWS, HID), preferred_element_type=F32
        )
    grad_pre = (grad * slope).astype(BF16)
    part = lax.dot_general(grad_pre, wh[...], (((1,), (1,)), ((), ())), preferred_element_type=F32)
    pgrad[...] = jnp.zeros((NC, OWN, LANES), F32)
    pgrad[:, :, 0:FEAT] = part.reshape(NC, OWN, FEAT)
    for i in range(1, NC):
        to = mod(c + i, NC)
        push(pgrad.at[to], rs5.at[i - 1], "rs5", (t, to))
    wait_recv(rs5, "rs5")
    total = pgrad[c]
    for i in range(NC - 1):
        total = total + rs5[i]
    halo[4] = total * 0.0625
    for i, (dt, dc) in enumerate(around):
        push(halo.at[4], halo.at[i if i < 4 else i + 1], "halo", (mod(t + dt, NT), mod(c + dc, NC)))

    wait_send(cols.at[0 : NC - 1], "ag1")
    wait_send(diff.at[0:8], "diff")
    wait_send(obs_recv.at[0 : NT - 1], "obs")
    wait_send(r1a, "r1a")
    wait_send(r1b, "r1b")
    wait_send(act.at[0 : NC - 1], "ag2")
    wait_send(r2a, "r2a")
    wait_send(r2b, "r2b")
    for way, steps in ways.items():
        for s in range(steps):
            ring_copy(s, way).wait_send()
    wait_send(g_all.at[:, 0], "core")
    wait_send(dep.at[0, 0:3, lo, :], "a1a")
    wait_send(dep.at[0, 0:3, hi, :], "a1b")
    wait_send(dep.at[0:3, :, lo, :], "a2a")
    wait_send(dep.at[0:3, :, hi, :], "a2b")
    wait_send(rs5, "rs5")

    strips[...] = jnp.zeros((3, 48, LANES), F32)
    wait_recv(halo.at[0:8], "halo")
    for dc in range(3):
        west, mid, east = (halo[8 - (dt * 3 + dc)] for dt in range(3))
        strips[dc, 6:8, :] = jnp.broadcast_to(west[7:8, :], (2, LANES))
        strips[dc, 40:42, :] = jnp.broadcast_to(east[0:1, :], (2, LANES))
        for j in range(OWN):
            strips[dc, 8 + 4 * j : 12 + 4 * j, :] = jnp.broadcast_to(mid[j : j + 1, :], (4, LANES))
    wait_send(halo.at[0:8], "halo")

    def swept(mine, before, after, i):
        here = root[:, i : i + 1]
        shape = (48, LANES)
        wide = lambda v: jnp.broadcast_to(v, shape)
        value = mine + wide(here * root[:, i + 1 : i + 2]) * (after - mine)
        value = value + wide(here * root[:, i - 1 : i]) * (before - mine)
        value = value + wide(to_east[:, i : i + 1]) * (pltpu.roll(mine, 47, 0) - mine)
        return value + wide(to_west[:, i : i + 1]) * (pltpu.roll(mine, 1, 0) - mine)

    band = lambda i: strips[0 if i < 2 else (1 if i < 6 else 2)]
    for i in range(1, 7):
        sweep[i - 1] = swept(band(i), band(i - 1), band(i + 1), i)
    for i in range(2, 6):
        out[i - 2] = swept(sweep[i - 1], sweep[i - 2], sweep[i], i)[8:40, 0:FEAT]


def body(fields, diffusivity, owners, observed, usable, w_hidden, b_hidden, w_radiance, b_radiance, inv_cov):
    vmem, hbm = pl.BlockSpec(memory_space=pltpu.VMEM), pl.BlockSpec(memory_space=pl.ANY)
    n = len(SEMS)
    return pl.pallas_call(
        kernel,
        out_shape=jax.ShapeDtypeStruct((4, 32, FEAT), F32),
        in_specs=[hbm, vmem, vmem, hbm, vmem, hbm, vmem, hbm, vmem, hbm],
        out_specs=vmem,
        scratch_shapes=[
            pltpu.VMEM((4, 32, FEAT), F32),
            pltpu.VMEM((4, 32, 128), F32),
            pltpu.VMEM((NT, CAP, CH), BF16),
            pltpu.VMEM((NT, CAP, CH), BF16),
            pltpu.VMEM((FEAT, HID), BF16),
            pltpu.VMEM((ALL_HID, CH), BF16),
            pltpu.VMEM((ROWS, CH), BF16),
            pltpu.VMEM((NC, OWN, LANES), BF16),
            pltpu.VMEM((NC, TC, HID), BF16),
            pltpu.VMEM((SIDE, SIDE, ROWS, HID), BF16),
            pltpu.VMEM((SIDE - 1, SIDE, HALF, HID), BF16),
            pltpu.VMEM((SIDE - 1, SIDE, HALF, HID), BF16),
            pltpu.VMEM((SIDE, HALF, HID), BF16),
            pltpu.VMEM((SIDE, HALF, HID), BF16),
            pltpu.VMEM((SIDE - 1, HALF, HID), BF16),
            pltpu.VMEM((SIDE - 1, HALF, HID), BF16),
            pltpu.VMEM((NZ, 2, ROWS, HID), BF16),
            pltpu.VMEM((SIDE, SIDE, TC, CH), BF16),
            pltpu.VMEM((NC, OWN, LANES), F32),
            pltpu.VMEM((NC - 1, OWN, LANES), F32),
            pltpu.VMEM((9, OWN, LANES), F32),
            pltpu.VMEM((9, 8, 128), F32),
            pltpu.VMEM((3, 48, LANES), F32),
            pltpu.VMEM((6, 48, LANES), F32),
            pltpu.SemaphoreType.DMA((6,)),
            pltpu.SemaphoreType.DMA((n,)),
            pltpu.SemaphoreType.DMA((n,)),
            pltpu.SemaphoreType.DMA((2, NZ // 2)),
            pltpu.SemaphoreType.DMA((2, NZ // 2)),
            pltpu.SemaphoreType.REGULAR,
        ],
        compiler_params=pltpu.CompilerParams(collective_id=0, has_side_effects=True),
    )(
        fields,
        diffusivity,
        owners.reshape(NT, TC),
        observed.reshape(NT, CAP, CH),
        usable.reshape(2, 128),
        w_hidden,
        b_hidden.reshape(1, HID),
        w_radiance,
        b_radiance.reshape(1, CH),
        inv_cov,
    )


def solution(mesh):
    placed = (
        P("chan", "tile", None), P("chan", "tile"), P(), P("tile", "chan"), P("tile"),
        P(None, "chan"), P("chan"), P(None, "chan"), P("chan"), P("tile", "chan"),
    )
    return jax.shard_map(
        body, mesh=mesh, in_specs=placed, out_specs=P("chan", "tile", None), check_vma=False
    )
```

```python
import jax
import jax.numpy as jnp
from jax import lax
from jax.experimental import pallas as pl
from jax.experimental.pallas import tpu as pltpu
from jax.sharding import PartitionSpec as P

MESH = pl.DeviceIdType.MESH
F32, BF16 = jnp.float32, jnp.bfloat16
NZ, SIDE, NC, NT = 16, 4, 16, 32
CAP = 8
OWN = 8
TC = 128
FEAT, LANES = 411, 512
HID, ALL_HID = 128, 2048
CH = 384
ROWS = 192
HALF = ROWS // 2
UNUSED = 2.0**100

SEMS = (
    "ag1", "ag2", "diff", "obs", "r1a", "r1b", "r2a", "r2b", "a1a", "a1b", "a2a", "a2b", "rs5", "halo",
)


STAGES = (
    ((0, 3), (0, -3), (0, 1), (0, -1)),
    ((-3, 3), (3, -3), (-3, 1), (3, -1), (-3, -1), (3, 1)),
    ((-6, 2), (-6, 1), (6, -1), (-6, -1), (6, 1)),
)


def kernel(
    fields_h, diff_in, owners_in, obs_h, usable_in, wh_h, bh_in, wr_h, br_in, ic_h,
    out,
    fields, quads, obs_send, obs_recv, wh, wr, ic,
    cols, act, gp, r1a, r1b, s1a, s1b, r2a, r2b, g_all, dep, pgrad, rs5, halo, diff, strips, sweep,
    local, send, recv, ring_s, ring_r, core_s, core_r, hello,
):
    t, c = lax.axis_index("tile"), lax.axis_index("chan")
    z, k = t // 2, t % 2
    y, x = c // SIDE, c % SIDE
    sem_of = {name: i for i, name in enumerate(SEMS)}

    def tile_at(dz, core):
        return lax.rem(z + dz + NZ, NZ) * 2 + core

    def mod(v, n):
        return lax.rem(v + n, n)

    def push(src, dst, name, where):
        i = sem_of[name]
        pltpu.make_async_remote_copy(
            src_ref=src, dst_ref=dst, send_sem=send.at[i], recv_sem=recv.at[i],
            device_id=where, device_id_type=MESH,
        ).start()

    lo, hi = slice(0, TC // 2), slice(TC // 2, TC)
    whole = {
        "ag1": cols.at[0 : NC - 1], "ag2": act.at[0 : NC - 1], "diff": diff.at[0:8], "obs": obs_recv.at[0 : NT - 1],
        "r1a": r1a, "r1b": r1b, "r2a": r2a, "r2b": r2b,
        "a1a": dep.at[0, 0:3, lo, :], "a1b": dep.at[0, 0:3, hi, :],
        "a2a": dep.at[0:3, :, lo, :], "a2b": dep.at[0:3, :, hi, :], "rs5": rs5, "halo": halo.at[0:8],
    }

    def wait_recv(name):
        pltpu.make_async_copy(whole[name], whole[name], recv.at[sem_of[name]]).wait()

    def wait_send(name):
        pltpu.make_async_copy(whole[name], whole[name], send.at[sem_of[name]]).wait()

    loads = [
        pltpu.make_async_copy(src, dst, local.at[i])
        for i, (src, dst) in enumerate(
            [(fields_h, fields), (ic_h, ic), (wr_h, wr), (obs_h, obs_send), (wh_h, wh)]
        )
    ]
    for copy in loads:
        copy.start()
    near = [(dz, core) for dz in (4, -4, 3, -3, 2, -2, 1, -1) for core in (0, 1)]
    around = [(dt, dc) for dt in (-1, 0, 1) for dc in (-1, 0, 1) if (dt, dc) != (0, 0)]
    barrier = pltpu.get_barrier_semaphore()
    greeted = [(t, mod(c + i, NC)) for i in range(1, NC)]
    greeted += [(tile_at(dz, core), c) for dz, core in near] + [(z * 2 + 1 - k, c)]
    greeted += [(mod(t + dt, NT), mod(c + dc, NC)) for dt, dc in around if dt and dc]
    for where in greeted:
        pl.semaphore_signal(barrier, inc=1, device_id=where, device_id_type=MESH)

    loads[0].wait()
    summed = fields[0] + fields[1] + fields[2] + fields[3]
    for b in range(LANES // 128):
        width = min(128, FEAT - b * 128)
        quads[b] = jnp.zeros((32, 128), F32)
        quads[b, :, 0:width] = summed[:, b * 128 : b * 128 + width]
        total = None
        for j in range(4):
            part = quads[b, pl.ds(j, OWN, stride=4), :]
            total = part if total is None else total + part
        cols[c, :, b * 128 : b * 128 + 128] = (total * 0.0625).astype(BF16)

    diff[4] = jnp.zeros((8, 128), F32)
    diff[4, 0:4, 0:32] = diff_in[...]

    pl.semaphore_wait(barrier, len(greeted))

    for i in range(1, NC):
        push(cols.at[c], cols.at[c], "ag1", (t, mod(c + i, NC)))
    for i, (dt, dc) in enumerate(around):
        push(diff.at[4], diff.at[i if i < 4 else i + 1], "diff", (mod(t + dt, NT), mod(c + dc, NC)))
    for step in (SIDE, -SIDE):
        pl.semaphore_signal(hello, inc=1, device_id=(tile_at(step, k), c), device_id_type=MESH)
    loads[3].wait()
    usable = usable_in[...].astype(F32)
    usable = jnp.transpose(jnp.concatenate([usable] * 4, axis=0))
    for h in range(2):
        part = slice(h * 16, h * 16 + 16)
        seen = obs_send[part].astype(F32).reshape(TC, CH)
        seen = jnp.where(usable[:, h : h + 1] > 0.5, seen, UNUSED)
        obs_send[part] = seen.reshape(16, CAP, CH).astype(BF16)

    own_obs = pltpu.make_async_copy(obs_send.at[t], obs_recv.at[t], local.at[5])
    own_obs.start()

    def send_obs(peers):
        for dz, core in peers:
            to = tile_at(dz, core)
            push(obs_send.at[to], obs_recv.at[t], "obs", (to, c))

    send_obs(near)
    send_obs([(0, 1 - k)])
    loads[1].wait()
    loads[2].wait()
    cov = ic[...]
    for b in range(NC // 2):
        part = lax.dot_general(
            cov, wr[b * 256 : b * 256 + 256, :], (((1,), (1,)), ((), ())), preferred_element_type=F32
        ).astype(BF16)
        for h in range(2):
            q = 2 * b + h
            gp[q // SIDE, q % SIDE] = part[:, h * 128 : h * 128 + 128]

    for d in range(1, SIDE):
        to_x, to_y = mod(x + d, SIDE), mod(y + d, SIDE)
        push(gp.at[:, to_x, 0:HALF, :], r1a.at[d - 1], "r1a", (t, y * SIDE + to_x))
        push(gp.at[to_y, :, HALF:ROWS, :], r1b.at[d - 1], "r1b", (t, to_y * SIDE + x))
    pl.semaphore_wait(hello, 2)
    send_obs([(dz, core) for dz in (8, 7, -7, 6, -6, 5, -5) for core in (0, 1)])

    own_row = jnp.broadcast_to(owners_in[pl.ds(t, 1), :].astype(F32), (TC, TC))
    own_col = jnp.transpose(own_row)
    at_row = lax.broadcasted_iota(jnp.int32, (TC, TC), 0)
    at_lane = lax.broadcasted_iota(jnp.int32, (TC, TC), 1)
    earlier = jnp.where((own_row == own_col) & (at_lane < at_row), 1.0, 0.0)
    rank = jnp.sum(earlier, axis=1, keepdims=True)
    slot = (own_col[:, 0:1] * float(CAP) + rank).astype(jnp.int32)
    select = jnp.where(
        slot == lax.broadcasted_iota(jnp.int32, (TC, NT * CAP), 1), 1.0, 0.0
    ).astype(BF16)

    loads[4].wait()
    wait_recv("ag1")
    tile_cols = cols[...].astype(F32).reshape(TC, LANES)[:, 0:FEAT].astype(BF16)
    preact = jnp.dot(tile_cols, wh[...], preferred_element_type=F32) + bh_in[...]
    squash = jax.nn.sigmoid(preact)
    act[c] = (preact * squash).astype(BF16)
    slope = squash * (1.0 + preact * (1.0 - squash))
    for i in range(1, NC):
        push(act.at[c], act.at[c], "ag2", (t, mod(c + i, NC)))

    def add(own, got):
        acc = own.astype(F32)
        for d in range(SIDE - 1):
            acc = acc + got[d].astype(F32)
        return acc.astype(BF16)

    wait_recv("r1a")
    s1a[...] = add(gp[:, x, 0:HALF, :], r1a)
    wait_recv("r1b")
    s1b[...] = add(gp[y, :, HALF:ROWS, :], r1b)
    for d in range(1, SIDE):
        to_x, to_y = mod(x + d, SIDE), mod(y + d, SIDE)
        push(s1a.at[to_y], r2a.at[d - 1], "r2a", (t, to_y * SIDE + x))
        push(s1b.at[to_x], r2b.at[d - 1], "r2b", (t, y * SIDE + to_x))
    def block_of(at, core):
        return g_all.at[mod(z + at, NZ), core]

    def along(stage, i):
        at, by = STAGES[stage][i]
        block = block_of(at, k)
        return pltpu.make_async_remote_copy(
            src_ref=block, dst_ref=block, send_sem=ring_s.at[stage, i], recv_sem=ring_r.at[stage, i],
            device_id=(tile_at(by, k), c), device_id_type=MESH,
        )

    def across(stage, i, core):
        at, by = STAGES[stage][i] if stage < 3 else (0, 0)
        block = block_of(at - by, core)
        return pltpu.make_async_remote_copy(
            src_ref=block, dst_ref=block, send_sem=core_s.at[stage, i], recv_sem=core_r.at[stage, i],
            device_id=(z * 2 + 1 - k, c), device_id_type=MESH,
        )

    def stage_in(stage):
        for i in range(len(STAGES[stage])):
            along(stage, i).wait_recv()
            if stage < 2:
                got = STAGES[stage][i][0] - STAGES[stage][i][1]
                for j, (at, by) in enumerate(STAGES[stage + 1]):
                    if at == got:
                        along(stage + 1, j).start()
        for i in range(len(STAGES[stage])):
            across(stage, i, k).start()

    wait_recv("r2a")
    g_all[z, k, 0:HALF, :] = add(s1a[y], r2a)
    wait_recv("r2b")
    g_all[z, k, HALF:ROWS, :] = add(s1b[x], r2b)
    for i in range(len(STAGES[0])):
        along(0, i).start()
    across(3, 0, k).start()

    wait_recv("ag2")
    tile_act = jnp.concatenate([act[i] for i in range(NC)], axis=1)
    radiance = jnp.dot(tile_act, wr[...], preferred_element_type=F32)
    radiance = radiance + jnp.concatenate([br_in[i : i + 1, :] for i in range(3)], axis=1)
    own_obs.wait()
    wait_recv("obs")
    arrived = obs_recv[...].astype(F32).reshape(NT * CAP, CH).astype(BF16)
    seen = jnp.dot(select, arrived, preferred_element_type=F32)
    dep[y, x] = jnp.where(seen < UNUSED * 0.5, radiance - seen, 0.0).astype(BF16)
    for d in range(1, SIDE):
        to_x, to_y = mod(x + d, SIDE), mod(y + d, SIDE)
        push(dep.at[y, x, lo, :], dep.at[y, x, lo, :], "a1a", (t, y * SIDE + to_x))
        push(dep.at[y, x, hi, :], dep.at[y, x, hi, :], "a1b", (t, to_y * SIDE + x))
    stage_in(0)
    wait_recv("a1a")
    for d in range(1, SIDE):
        push(dep.at[y, :, lo, :], dep.at[y, :, lo, :], "a2a", (t, mod(y + d, SIDE) * SIDE + x))
    wait_recv("a1b")
    for d in range(1, SIDE):
        push(dep.at[:, x, hi, :], dep.at[:, x, hi, :], "a2b", (t, y * SIDE + mod(x + d, SIDE)))
    stage_in(1)

    wait_recv("diff")
    lane = lax.broadcasted_iota(jnp.int32, (8, 128), 1)
    row = lax.broadcasted_iota(jnp.int32, (8, 128), 0)
    bands = []
    for dc in range(3):
        west, mid, east = (diff[8 - (dt * 3 + dc)] for dt in range(3))
        bands.append(
            jnp.where(
                lane < 8,
                pltpu.roll(west, 104, 1),
                jnp.where(lane < 40, pltpu.roll(mid, 8, 1), pltpu.roll(east, 40, 1)),
            )
        )
    upper = jnp.where(c > 0, pltpu.roll(bands[0], 6, 0), 0.0)
    lower = jnp.where(c < NC - 1, pltpu.roll(bands[2], 6, 0), 0.0)
    root = jnp.where(row < 2, upper, jnp.where(row < 6, pltpu.roll(bands[1], 2, 0), lower))
    root = jnp.sqrt(jnp.where((lane < 6) | (lane > 41), 0.0, root))
    root = jnp.transpose(root)[0:48, :]
    to_east = root * pltpu.roll(root, 47, 0)
    to_west = root * pltpu.roll(root, 1, 0)

    wait_recv("a2a")
    wait_recv("a2b")
    grad = jnp.zeros((TC, HID), F32)
    for stage in (3, 0, 1, 2):
        entries = STAGES[stage] if stage < 3 else ((0, 0),)
        if stage == 2:
            stage_in(2)
        for i, (at, by) in enumerate(entries):
            across(stage, i, 1 - k).wait_recv()
            block = mod(z + at - by, NZ)
            grad = grad + jnp.dot(
                dep[block // SIDE, lax.rem(block, SIDE)],
                g_all[block].reshape(2 * ROWS, HID),
                preferred_element_type=F32,
            )
    grad_pre = (grad * slope).astype(BF16)
    part = lax.dot_general(grad_pre, wh[...], (((1,), (1,)), ((), ())), preferred_element_type=F32)
    pgrad[...] = jnp.zeros((NC, OWN, LANES), F32)
    pgrad[:, :, 0:FEAT] = part.reshape(NC, OWN, FEAT)
    for i in range(1, NC):
        to = mod(c + i, NC)
        push(pgrad.at[to], rs5.at[i - 1], "rs5", (t, to))
    wait_recv("rs5")
    total = pgrad[c]
    for i in range(NC - 1):
        total = total + rs5[i]
    halo[4] = total * 0.0625
    for i, (dt, dc) in enumerate(around):
        push(halo.at[4], halo.at[i if i < 4 else i + 1], "halo", (mod(t + dt, NT), mod(c + dc, NC)))

    for name in SEMS[:-1]:
        wait_send(name)
    for stage, entries in enumerate(STAGES):
        for i in range(len(entries)):
            along(stage, i).wait_send()
            across(stage, i, k).wait_send()
    across(3, 0, k).wait_send()

    strips[...] = jnp.zeros((3, 48, LANES), F32)
    wait_recv("halo")
    for dc in range(3):
        west, mid, east = (halo[8 - (dt * 3 + dc)] for dt in range(3))
        strips[dc, 6:8, :] = jnp.broadcast_to(west[7:8, :], (2, LANES))
        strips[dc, 40:42, :] = jnp.broadcast_to(east[0:1, :], (2, LANES))
        for j in range(OWN):
            strips[dc, 8 + 4 * j : 12 + 4 * j, :] = jnp.broadcast_to(mid[j : j + 1, :], (4, LANES))
    wait_send("halo")

    def swept(mine, before, after, i):
        here = root[:, i : i + 1]
        shape = (48, LANES)
        wide = lambda v: jnp.broadcast_to(v, shape)
        value = mine + wide(here * root[:, i + 1 : i + 2]) * (after - mine)
        value = value + wide(here * root[:, i - 1 : i]) * (before - mine)
        value = value + wide(to_east[:, i : i + 1]) * (pltpu.roll(mine, 47, 0) - mine)
        return value + wide(to_west[:, i : i + 1]) * (pltpu.roll(mine, 1, 0) - mine)

    band = lambda i: strips[0 if i < 2 else (1 if i < 6 else 2)]
    for i in range(1, 7):
        sweep[i - 1] = swept(band(i), band(i - 1), band(i + 1), i)
    for i in range(2, 6):
        out[i - 2] = swept(sweep[i - 1], sweep[i - 2], sweep[i], i)[8:40, 0:FEAT]


def body(fields, diffusivity, owners, observed, usable, w_hidden, b_hidden, w_radiance, b_radiance, inv_cov):
    vmem, hbm = pl.BlockSpec(memory_space=pltpu.VMEM), pl.BlockSpec(memory_space=pl.ANY)
    n = len(SEMS)
    return pl.pallas_call(
        kernel,
        out_shape=jax.ShapeDtypeStruct((4, 32, FEAT), F32),
        in_specs=[hbm, vmem, vmem, hbm, vmem, hbm, vmem, hbm, vmem, hbm],
        out_specs=vmem,
        scratch_shapes=[
            pltpu.VMEM((4, 32, FEAT), F32),
            pltpu.VMEM((4, 32, 128), F32),
            pltpu.VMEM((NT, CAP, CH), BF16),
            pltpu.VMEM((NT, CAP, CH), BF16),
            pltpu.VMEM((FEAT, HID), BF16),
            pltpu.VMEM((ALL_HID, CH), BF16),
            pltpu.VMEM((ROWS, CH), BF16),
            pltpu.VMEM((NC, OWN, LANES), BF16),
            pltpu.VMEM((NC, TC, HID), BF16),
            pltpu.VMEM((SIDE, SIDE, ROWS, HID), BF16),
            pltpu.VMEM((SIDE - 1, SIDE, HALF, HID), BF16),
            pltpu.VMEM((SIDE - 1, SIDE, HALF, HID), BF16),
            pltpu.VMEM((SIDE, HALF, HID), BF16),
            pltpu.VMEM((SIDE, HALF, HID), BF16),
            pltpu.VMEM((SIDE - 1, HALF, HID), BF16),
            pltpu.VMEM((SIDE - 1, HALF, HID), BF16),
            pltpu.VMEM((NZ, 2, ROWS, HID), BF16),
            pltpu.VMEM((SIDE, SIDE, TC, CH), BF16),
            pltpu.VMEM((NC, OWN, LANES), F32),
            pltpu.VMEM((NC - 1, OWN, LANES), F32),
            pltpu.VMEM((9, OWN, LANES), F32),
            pltpu.VMEM((9, 8, 128), F32),
            pltpu.VMEM((3, 48, LANES), F32),
            pltpu.VMEM((6, 48, LANES), F32),
            pltpu.SemaphoreType.DMA((6,)),
            pltpu.SemaphoreType.DMA((n,)),
            pltpu.SemaphoreType.DMA((n,)),
            pltpu.SemaphoreType.DMA((3, 6)),
            pltpu.SemaphoreType.DMA((3, 6)),
            pltpu.SemaphoreType.DMA((4, 6)),
            pltpu.SemaphoreType.DMA((4, 6)),
            pltpu.SemaphoreType.REGULAR,
        ],
        compiler_params=pltpu.CompilerParams(collective_id=0, has_side_effects=True),
    )(
        fields,
        diffusivity,
        owners.reshape(NT, TC),
        observed.reshape(NT, CAP, CH),
        usable.reshape(2, 128),
        w_hidden,
        b_hidden.reshape(1, HID),
        w_radiance,
        b_radiance.reshape(3, 128),
        inv_cov,
    )


def solution(mesh):
    placed = (
        P("chan", "tile", None), P("chan", "tile"), P(), P("tile", "chan"), P("tile"),
        P(None, "chan"), P("chan"), P(None, "chan"), P("chan"), P("tile", "chan"),
    )
    return jax.shard_map(
        body, mesh=mesh, in_specs=placed, out_specs=P("chan", "tile", None), check_vma=False
    )
```

```python
import jax
import jax.numpy as jnp
from jax import lax
from jax.experimental import pallas as pl
from jax.experimental.pallas import tpu as pltpu
from jax.sharding import PartitionSpec as P

MESH = pl.DeviceIdType.MESH
F32, BF16 = jnp.float32, jnp.bfloat16
NZ, SIDE, NC, NT = 16, 4, 16, 32
CAP = 8
OWN = 8
TC = 128
FEAT, LANES = 411, 512
HID, ALL_HID = 128, 2048
CH = 384
ROWS = 192
HALF = ROWS // 2
UNUSED = 2.0**100

SEMS = (
    "ag1", "diff", "obs", "r1a", "r1b", "r2a", "r2b", "rs5", "halo",
    *(who + part for who in ("act", "dep") for part in ("x1", "x2", "x3", "y1", "y2", "y3", "over_y", "over_x")),
)
STAGES = (
    ((0, 3), (0, -3), (0, 1), (0, -1)),
    ((-3, 3), (3, -3), (-3, 1), (3, -1), (-3, -1), (3, 1)),
    ((-6, 2), (-6, 1), (6, -1), (-6, -1), (6, 1)),
)


def kernel(
    fields_h, diff_in, owners_in, obs_h, usable_in, wh_h, bh_in, wr_h, br_in, ic_h,
    out,
    fields, quads, obs_send, obs_recv, wh, wr, ic,
    cols, act, gp, r1a, r1b, s1a, s1b, r2a, r2b, g_all, dep, pgrad, rs5, halo, diff, strips, sweep,
    local, send, recv, ring_s, ring_r, core_s, core_r, hello,
):
    t, c = lax.axis_index("tile"), lax.axis_index("chan")
    z, k = t // 2, t % 2
    y, x = c // SIDE, c % SIDE
    sem_of = {name: i for i, name in enumerate(SEMS)}

    def tile_at(dz, core):
        return lax.rem(z + dz + NZ, NZ) * 2 + core

    def mod(v, n):
        return lax.rem(v + n, n)

    def push(src, dst, name, where):
        i = sem_of[name]
        pltpu.make_async_remote_copy(
            src_ref=src, dst_ref=dst, send_sem=send.at[i], recv_sem=recv.at[i],
            device_id=where, device_id_type=MESH,
        ).start()

    lo, hi = slice(0, TC // 2), slice(TC // 2, TC)
    whole = {
        "ag1": cols.at[0 : NC - 1], "diff": diff.at[0:8], "obs": obs_recv.at[0 : NT - 1],
        "r1a": r1a, "r1b": r1b, "r2a": r2a, "r2b": r2b, "rs5": rs5, "halo": halo.at[0:8],
    }
    blocks_of = {"act": act, "dep": dep}
    for who, buf in blocks_of.items():
        for d in range(1, SIDE):
            whole[f"{who}x{d}"] = buf.at[0, 0, lo, :]
            whole[f"{who}y{d}"] = buf.at[0, 0, hi, :]
        whole[who + "over_y"] = buf.at[0:3, :, lo, :]
        whole[who + "over_x"] = buf.at[0:3, :, hi, :]

    def wait_recv(name):
        pltpu.make_async_copy(whole[name], whole[name], recv.at[sem_of[name]]).wait()

    def wait_send(name):
        pltpu.make_async_copy(whole[name], whole[name], send.at[sem_of[name]]).wait()

    def over_y(who, xx):
        block = blocks_of[who].at[y, xx, lo, :]
        for d in (2, 1, 3):
            push(block, block, who + "over_y", (t, mod(y + d, SIDE) * SIDE + x))

    def over_x(who, yy):
        block = blocks_of[who].at[yy, x, hi, :]
        for d in (2, 1, 3):
            push(block, block, who + "over_x", (t, y * SIDE + mod(x + d, SIDE)))

    def gather(who):
        upper, lower = blocks_of[who].at[y, x, lo, :], blocks_of[who].at[y, x, hi, :]
        for d in (2, 1, 3):
            push(upper, upper, f"{who}x{d}", (t, y * SIDE + mod(x + d, SIDE)))
            push(lower, lower, f"{who}y{d}", (t, mod(y + d, SIDE) * SIDE + x))
        over_y(who, x)
        over_x(who, y)

    def relay(who, *steps):
        for d in steps:
            wait_recv(f"{who}x{d}")
            over_y(who, mod(x - d, SIDE))
            wait_recv(f"{who}y{d}")
            over_x(who, mod(y - d, SIDE))

    def gathered(who):
        wait_recv(who + "over_y")
        wait_recv(who + "over_x")

    loads = [
        pltpu.make_async_copy(src, dst, local.at[i])
        for i, (src, dst) in enumerate(
            [(fields_h, fields), (ic_h, ic), (wr_h, wr), (obs_h, obs_send), (wh_h, wh)]
        )
    ]
    for copy in loads:
        copy.start()
    near = [(dz, core) for dz in (4, -4, 3, -3, 2, -2, 1, -1) for core in (0, 1)]
    around = [(dt, dc) for dt in (-1, 0, 1) for dc in (-1, 0, 1) if (dt, dc) != (0, 0)]
    barrier = pltpu.get_barrier_semaphore()
    greeted = [(t, mod(c + i, NC)) for i in range(1, NC)]
    greeted += [(tile_at(dz, core), c) for dz, core in near] + [(z * 2 + 1 - k, c)]
    greeted += [(mod(t + dt, NT), mod(c + dc, NC)) for dt, dc in around if dt and dc]
    for where in greeted:
        pl.semaphore_signal(barrier, inc=1, device_id=where, device_id_type=MESH)

    loads[0].wait()
    summed = fields[0] + fields[1] + fields[2] + fields[3]
    for b in range(LANES // 128):
        width = min(128, FEAT - b * 128)
        quads[b] = jnp.zeros((32, 128), F32)
        quads[b, :, 0:width] = summed[:, b * 128 : b * 128 + width]
        total = None
        for j in range(4):
            part = quads[b, pl.ds(j, OWN, stride=4), :]
            total = part if total is None else total + part
        cols[c, :, b * 128 : b * 128 + 128] = (total * 0.0625).astype(BF16)

    diff[4] = jnp.zeros((8, 128), F32)
    diff[4, 0:4, 0:32] = diff_in[...]

    loads[1].wait()
    loads[2].wait()
    cov = ic[...]
    for b in range(NC // 2):
        part = lax.dot_general(
            cov, wr[b * 256 : b * 256 + 256, :], (((1,), (1,)), ((), ())), preferred_element_type=F32
        ).astype(BF16)
        for h in range(2):
            q = 2 * b + h
            gp[q // SIDE, q % SIDE] = part[:, h * 128 : h * 128 + 128]

    pl.semaphore_wait(barrier, len(greeted))

    for i in range(1, NC):
        push(cols.at[c], cols.at[c], "ag1", (t, mod(c + i, NC)))
    for i, (dt, dc) in enumerate(around):
        push(diff.at[4], diff.at[i if i < 4 else i + 1], "diff", (mod(t + dt, NT), mod(c + dc, NC)))
    for step in (SIDE, -SIDE):
        pl.semaphore_signal(hello, inc=1, device_id=(tile_at(step, k), c), device_id_type=MESH)
    loads[3].wait()
    usable = usable_in[...].astype(F32)
    usable = jnp.transpose(jnp.concatenate([usable] * 4, axis=0))
    for h in range(2):
        part = slice(h * 16, h * 16 + 16)
        seen = obs_send[part].astype(F32).reshape(TC, CH)
        seen = jnp.where(usable[:, h : h + 1] > 0.5, seen, UNUSED)
        obs_send[part] = seen.reshape(16, CAP, CH).astype(BF16)

    own_obs = pltpu.make_async_copy(obs_send.at[t], obs_recv.at[t], local.at[5])
    own_obs.start()

    def send_obs(peers):
        for dz, core in peers:
            to = tile_at(dz, core)
            push(obs_send.at[to], obs_recv.at[t], "obs", (to, c))

    send_obs(near)
    send_obs([(0, 1 - k)])
    for d in range(1, SIDE):
        to_x, to_y = mod(x + d, SIDE), mod(y + d, SIDE)
        push(gp.at[:, to_x, 0:HALF, :], r1a.at[d - 1], "r1a", (t, y * SIDE + to_x))
        push(gp.at[to_y, :, HALF:ROWS, :], r1b.at[d - 1], "r1b", (t, to_y * SIDE + x))
    pl.semaphore_wait(hello, 2)
    send_obs([(dz, core) for dz in (8, 7, -7, 6, -6, 5, -5) for core in (0, 1)])

    own_row = jnp.broadcast_to(owners_in[pl.ds(t, 1), :].astype(F32), (TC, TC))
    own_col = jnp.transpose(own_row)
    at_row = lax.broadcasted_iota(jnp.int32, (TC, TC), 0)
    at_lane = lax.broadcasted_iota(jnp.int32, (TC, TC), 1)
    earlier = jnp.where((own_row == own_col) & (at_lane < at_row), 1.0, 0.0)
    rank = jnp.sum(earlier, axis=1, keepdims=True)
    slot = (own_col[:, 0:1] * float(CAP) + rank).astype(jnp.int32)
    select = jnp.where(
        slot == lax.broadcasted_iota(jnp.int32, (TC, NT * CAP), 1), 1.0, 0.0
    ).astype(BF16)

    loads[4].wait()
    wait_recv("ag1")
    tile_cols = cols[...].astype(F32).reshape(TC, LANES)[:, 0:FEAT].astype(BF16)
    preact = jnp.dot(tile_cols, wh[...], preferred_element_type=F32) + bh_in[...]
    squash = jax.nn.sigmoid(preact)
    act[y, x] = (preact * squash).astype(BF16)
    slope = squash * (1.0 + preact * (1.0 - squash))
    gather("act")

    def add(own, got):
        acc = own.astype(F32)
        for d in range(SIDE - 1):
            acc = acc + got[d].astype(F32)
        return acc.astype(BF16)

    wait_recv("r1a")
    s1a[...] = add(gp[:, x, 0:HALF, :], r1a)
    wait_recv("r1b")
    s1b[...] = add(gp[y, :, HALF:ROWS, :], r1b)
    for d in range(1, SIDE):
        to_x, to_y = mod(x + d, SIDE), mod(y + d, SIDE)
        push(s1a.at[to_y], r2a.at[d - 1], "r2a", (t, to_y * SIDE + x))
        push(s1b.at[to_x], r2b.at[d - 1], "r2b", (t, y * SIDE + to_x))
    def block_of(at, core):
        return g_all.at[mod(z + at, NZ), core]

    def along(stage, i):
        at, by = STAGES[stage][i]
        block = block_of(at, k)
        return pltpu.make_async_remote_copy(
            src_ref=block, dst_ref=block, send_sem=ring_s.at[stage, i], recv_sem=ring_r.at[stage, i],
            device_id=(tile_at(by, k), c), device_id_type=MESH,
        )

    def across(stage, i, core):
        at, by = STAGES[stage][i] if stage < 3 else (0, 0)
        block = block_of(at - by, core)
        return pltpu.make_async_remote_copy(
            src_ref=block, dst_ref=block, send_sem=core_s.at[stage, i], recv_sem=core_r.at[stage, i],
            device_id=(z * 2 + 1 - k, c), device_id_type=MESH,
        )

    def stage_in(stage):
        for i in range(len(STAGES[stage])):
            along(stage, i).wait_recv()
            if stage < 2:
                got = STAGES[stage][i][0] - STAGES[stage][i][1]
                for j, (at, by) in enumerate(STAGES[stage + 1]):
                    if at == got:
                        along(stage + 1, j).start()
            across(stage, i, k).start()

    relay("act", 1, 3, 2)
    wait_recv("r2a")
    g_all[z, k, 0:HALF, :] = add(s1a[y], r2a)
    wait_recv("r2b")
    g_all[z, k, HALF:ROWS, :] = add(s1b[x], r2b)
    for i in range(len(STAGES[0])):
        along(0, i).start()
    across(3, 0, k).start()

    gathered("act")
    tile_act = jnp.concatenate([act[i // SIDE, i % SIDE] for i in range(NC)], axis=1)
    radiance = jnp.dot(tile_act, wr[...], preferred_element_type=F32)
    radiance = radiance + jnp.concatenate([br_in[i : i + 1, :] for i in range(3)], axis=1)
    own_obs.wait()
    wait_recv("obs")
    arrived = obs_recv[...].astype(F32).reshape(NT * CAP, CH).astype(BF16)
    seen = jnp.dot(select, arrived, preferred_element_type=F32)
    dep[y, x] = jnp.where(seen < UNUSED * 0.5, radiance - seen, 0.0).astype(BF16)
    gather("dep")
    relay("dep", 1, 3)
    stage_in(0)
    relay("dep", 2)
    stage_in(1)

    wait_recv("diff")
    lane = lax.broadcasted_iota(jnp.int32, (8, 128), 1)
    row = lax.broadcasted_iota(jnp.int32, (8, 128), 0)
    bands = []
    for dc in range(3):
        west, mid, east = (diff[8 - (dt * 3 + dc)] for dt in range(3))
        bands.append(
            jnp.where(
                lane < 8,
                pltpu.roll(west, 104, 1),
                jnp.where(lane < 40, pltpu.roll(mid, 8, 1), pltpu.roll(east, 40, 1)),
            )
        )
    upper = jnp.where(c > 0, pltpu.roll(bands[0], 6, 0), 0.0)
    lower = jnp.where(c < NC - 1, pltpu.roll(bands[2], 6, 0), 0.0)
    root = jnp.where(row < 2, upper, jnp.where(row < 6, pltpu.roll(bands[1], 2, 0), lower))
    root = jnp.sqrt(jnp.where((lane < 6) | (lane > 41), 0.0, root))
    root = jnp.transpose(root)[0:48, :]
    to_east = root * pltpu.roll(root, 47, 0)
    to_west = root * pltpu.roll(root, 1, 0)

    gathered("dep")
    grad = jnp.zeros((TC, HID), F32)
    for stage in (3, 0, 1, 2):
        entries = STAGES[stage] if stage < 3 else ((0, 0),)
        if stage == 2:
            stage_in(2)
        for i, (at, by) in enumerate(entries):
            across(stage, i, 1 - k).wait_recv()
            block = mod(z + at - by, NZ)
            grad = grad + jnp.dot(
                dep[block // SIDE, lax.rem(block, SIDE)],
                g_all[block].reshape(2 * ROWS, HID),
                preferred_element_type=F32,
            )
    grad_pre = (grad * slope).astype(BF16)
    part = lax.dot_general(grad_pre, wh[...], (((1,), (1,)), ((), ())), preferred_element_type=F32)
    pgrad[...] = jnp.zeros((NC, OWN, LANES), F32)
    pgrad[:, :, 0:FEAT] = part.reshape(NC, OWN, FEAT)
    for i in range(1, NC):
        to = mod(c + i, NC)
        push(pgrad.at[to], rs5.at[i - 1], "rs5", (t, to))
    wait_recv("rs5")
    total = pgrad[c]
    for i in range(NC - 1):
        total = total + rs5[i]
    halo[4] = total * 0.0625
    for i, (dt, dc) in enumerate(around):
        push(halo.at[4], halo.at[i if i < 4 else i + 1], "halo", (mod(t + dt, NT), mod(c + dc, NC)))

    for name in SEMS:
        if name != "halo":
            wait_send(name)
    for stage, entries in enumerate(STAGES):
        for i in range(len(entries)):
            along(stage, i).wait_send()
            across(stage, i, k).wait_send()
    across(3, 0, k).wait_send()

    strips[...] = jnp.zeros((3, 48, LANES), F32)
    wait_recv("halo")
    for dc in range(3):
        west, mid, east = (halo[8 - (dt * 3 + dc)] for dt in range(3))
        strips[dc, 6:8, :] = jnp.broadcast_to(west[7:8, :], (2, LANES))
        strips[dc, 40:42, :] = jnp.broadcast_to(east[0:1, :], (2, LANES))
        for j in range(OWN):
            strips[dc, 8 + 4 * j : 12 + 4 * j, :] = jnp.broadcast_to(mid[j : j + 1, :], (4, LANES))
    wait_send("halo")

    def swept(mine, before, after, i):
        here = root[:, i : i + 1]
        shape = (48, LANES)
        wide = lambda v: jnp.broadcast_to(v, shape)
        value = mine + wide(here * root[:, i + 1 : i + 2]) * (after - mine)
        value = value + wide(here * root[:, i - 1 : i]) * (before - mine)
        value = value + wide(to_east[:, i : i + 1]) * (pltpu.roll(mine, 47, 0) - mine)
        return value + wide(to_west[:, i : i + 1]) * (pltpu.roll(mine, 1, 0) - mine)

    band = lambda i: strips[0 if i < 2 else (1 if i < 6 else 2)]
    for i in range(1, 7):
        sweep[i - 1] = swept(band(i), band(i - 1), band(i + 1), i)
    for i in range(2, 6):
        out[i - 2] = swept(sweep[i - 1], sweep[i - 2], sweep[i], i)[8:40, 0:FEAT]


def body(fields, diffusivity, owners, observed, usable, w_hidden, b_hidden, w_radiance, b_radiance, inv_cov):
    vmem, hbm = pl.BlockSpec(memory_space=pltpu.VMEM), pl.BlockSpec(memory_space=pl.ANY)
    n = len(SEMS)
    return pl.pallas_call(
        kernel,
        out_shape=jax.ShapeDtypeStruct((4, 32, FEAT), F32),
        in_specs=[hbm, vmem, vmem, hbm, vmem, hbm, vmem, hbm, vmem, hbm],
        out_specs=vmem,
        scratch_shapes=[
            pltpu.VMEM((4, 32, FEAT), F32),
            pltpu.VMEM((4, 32, 128), F32),
            pltpu.VMEM((NT, CAP, CH), BF16),
            pltpu.VMEM((NT, CAP, CH), BF16),
            pltpu.VMEM((FEAT, HID), BF16),
            pltpu.VMEM((ALL_HID, CH), BF16),
            pltpu.VMEM((ROWS, CH), BF16),
            pltpu.VMEM((NC, OWN, LANES), BF16),
            pltpu.VMEM((SIDE, SIDE, TC, HID), BF16),
            pltpu.VMEM((SIDE, SIDE, ROWS, HID), BF16),
            pltpu.VMEM((SIDE - 1, SIDE, HALF, HID), BF16),
            pltpu.VMEM((SIDE - 1, SIDE, HALF, HID), BF16),
            pltpu.VMEM((SIDE, HALF, HID), BF16),
            pltpu.VMEM((SIDE, HALF, HID), BF16),
            pltpu.VMEM((SIDE - 1, HALF, HID), BF16),
            pltpu.VMEM((SIDE - 1, HALF, HID), BF16),
            pltpu.VMEM((NZ, 2, ROWS, HID), BF16),
            pltpu.VMEM((SIDE, SIDE, TC, CH), BF16),
            pltpu.VMEM((NC, OWN, LANES), F32),
            pltpu.VMEM((NC - 1, OWN, LANES), F32),
            pltpu.VMEM((9, OWN, LANES), F32),
            pltpu.VMEM((9, 8, 128), F32),
            pltpu.VMEM((3, 48, LANES), F32),
            pltpu.VMEM((6, 48, LANES), F32),
            pltpu.SemaphoreType.DMA((6,)),
            pltpu.SemaphoreType.DMA((n,)),
            pltpu.SemaphoreType.DMA((n,)),
            pltpu.SemaphoreType.DMA((3, 6)),
            pltpu.SemaphoreType.DMA((3, 6)),
            pltpu.SemaphoreType.DMA((4, 6)),
            pltpu.SemaphoreType.DMA((4, 6)),
            pltpu.SemaphoreType.REGULAR,
        ],
        compiler_params=pltpu.CompilerParams(collective_id=0, has_side_effects=True),
    )(
        fields,
        diffusivity,
        owners.reshape(NT, TC),
        observed.reshape(NT, CAP, CH),
        usable.reshape(2, 128),
        w_hidden,
        b_hidden.reshape(1, HID),
        w_radiance,
        b_radiance.reshape(3, 128),
        inv_cov,
    )


def solution(mesh):
    placed = (
        P("chan", "tile", None), P("chan", "tile"), P(), P("tile", "chan"), P("tile"),
        P(None, "chan"), P("chan"), P(None, "chan"), P("chan"), P("tile", "chan"),
    )
    return jax.shard_map(
        body, mesh=mesh, in_specs=placed, out_specs=P("chan", "tile", None), check_vma=False
    )
```

```python
import jax
import jax.numpy as jnp
from jax import lax
from jax.experimental import pallas as pl
from jax.experimental.pallas import tpu as pltpu
from jax.sharding import PartitionSpec as P

MESH = pl.DeviceIdType.MESH
F32, BF16 = jnp.float32, jnp.bfloat16
NZ, SIDE, NC, NT = 16, 4, 16, 32
CAP = 8
OWN = 8
TC = 128
FEAT, LANES = 411, 512
HID, ALL_HID = 128, 2048
CH = 384
ROWS = 192
HALF = ROWS // 2
UNUSED = 2.0**100

SEMS = (
    "ag1", "diff", "obs", "r1a", "r1b", "r2a", "r2b", "rs5", "halo",
    *(who + part for who in ("act", "dep") for part in ("x1", "x2", "x3", "y1", "y2", "y3", "over_y", "over_x")),
)
STAGES = (
    ((0, 3), (0, -3), (0, 1), (0, -1)),
    ((-3, 3), (3, -3), (-3, 1), (3, -1), (-3, -1), (3, 1)),
    ((-6, 2), (-6, 1), (6, -1), (-6, -1), (6, 1)),
)


def kernel(
    fields_h, diff_in, owners_in, obs_h, usable_in, wh_h, bh_in, wr_h, br_in, ic_h,
    out,
    fields, quads, obs_send, obs_recv, wh, wr, ic,
    cols, act, gp, r1a, r1b, s1a, s1b, r2a, r2b, g_all, dep, pgrad, rs5, halo, diff, strips, sweep,
    local, send, recv, ring_s, ring_r, core_s, core_r, hello,
):
    t, c = lax.axis_index("tile"), lax.axis_index("chan")
    z, k = t // 2, t % 2
    y, x = c // SIDE, c % SIDE
    sem_of = {name: i for i, name in enumerate(SEMS)}

    def tile_at(dz, core):
        return lax.rem(z + dz + NZ, NZ) * 2 + core

    def mod(v, n):
        return lax.rem(v + n, n)

    def push(src, dst, name, where):
        i = sem_of[name]
        pltpu.make_async_remote_copy(
            src_ref=src, dst_ref=dst, send_sem=send.at[i], recv_sem=recv.at[i],
            device_id=where, device_id_type=MESH,
        ).start()

    lo, hi = slice(0, TC // 2), slice(TC // 2, TC)
    whole = {
        "ag1": cols.at[0 : NC - 1], "diff": diff.at[0:8], "obs": obs_recv.at[0 : NT - 1],
        "r1a": r1a, "r1b": r1b, "r2a": r2a, "r2b": r2b, "rs5": rs5, "halo": halo.at[0:8],
    }
    blocks_of = {"act": act, "dep": dep}
    for who, buf in blocks_of.items():
        for d in range(1, SIDE):
            whole[f"{who}x{d}"] = buf.at[0, 0, lo, :]
            whole[f"{who}y{d}"] = buf.at[0, 0, hi, :]
        whole[who + "over_y"] = buf.at[0:3, :, lo, :]
        whole[who + "over_x"] = buf.at[0:3, :, hi, :]

    def wait_recv(name):
        pltpu.make_async_copy(whole[name], whole[name], recv.at[sem_of[name]]).wait()

    def wait_send(name):
        pltpu.make_async_copy(whole[name], whole[name], send.at[sem_of[name]]).wait()

    def over_y(who, xx):
        block = blocks_of[who].at[y, xx, lo, :]
        for d in (2, 1, 3):
            push(block, block, who + "over_y", (t, mod(y + d, SIDE) * SIDE + x))

    def over_x(who, yy):
        block = blocks_of[who].at[yy, x, hi, :]
        for d in (2, 1, 3):
            push(block, block, who + "over_x", (t, y * SIDE + mod(x + d, SIDE)))

    def gather(who):
        upper, lower = blocks_of[who].at[y, x, lo, :], blocks_of[who].at[y, x, hi, :]
        for d in (2, 1, 3):
            push(upper, upper, f"{who}x{d}", (t, y * SIDE + mod(x + d, SIDE)))
            push(lower, lower, f"{who}y{d}", (t, mod(y + d, SIDE) * SIDE + x))
        over_y(who, x)
        over_x(who, y)

    def relay(who, *steps):
        for d in steps:
            wait_recv(f"{who}x{d}")
            over_y(who, mod(x - d, SIDE))
            wait_recv(f"{who}y{d}")
            over_x(who, mod(y - d, SIDE))

    def gathered(who):
        wait_recv(who + "over_y")
        wait_recv(who + "over_x")

    loads = [
        pltpu.make_async_copy(src, dst, local.at[i])
        for i, (src, dst) in enumerate(
            [(fields_h, fields), (ic_h, ic), (wr_h, wr), (obs_h, obs_send), (wh_h, wh)]
        )
    ]
    for copy in loads:
        copy.start()
    near = [(dz, core) for dz in (4, -4, 3, -3, 2, -2, 1, -1) for core in (0, 1)]
    around = [(dt, dc) for dt in (-1, 0, 1) for dc in (-1, 0, 1) if (dt, dc) != (0, 0)]
    barrier = pltpu.get_barrier_semaphore()
    greeted = [(t, mod(c + i, NC)) for i in range(1, NC)]
    greeted += [(tile_at(dz, core), c) for dz, core in near] + [(z * 2 + 1 - k, c)]
    greeted += [(mod(t + dt, NT), mod(c + dc, NC)) for dt, dc in around if dt and dc]
    for where in greeted:
        pl.semaphore_signal(barrier, inc=1, device_id=where, device_id_type=MESH)

    loads[0].wait()
    summed = fields[0] + fields[1] + fields[2] + fields[3]
    for b in range(LANES // 128):
        width = min(128, FEAT - b * 128)
        quads[b] = jnp.zeros((32, 128), F32)
        quads[b, :, 0:width] = summed[:, b * 128 : b * 128 + width]
        total = None
        for j in range(4):
            part = quads[b, pl.ds(j, OWN, stride=4), :]
            total = part if total is None else total + part
        cols[c, :, b * 128 : b * 128 + 128] = (total * 0.0625).astype(BF16)

    diff[4] = jnp.zeros((8, 128), F32)
    diff[4, 0:4, 0:32] = diff_in[...]

    loads[1].wait()
    loads[2].wait()
    cov = ic[...]
    for b in range(NC // 2):
        part = lax.dot_general(
            cov, wr[b * 256 : b * 256 + 256, :], (((1,), (1,)), ((), ())), preferred_element_type=F32
        ).astype(BF16)
        for h in range(2):
            q = 2 * b + h
            gp[q // SIDE, q % SIDE] = part[:, h * 128 : h * 128 + 128]

    pl.semaphore_wait(barrier, len(greeted))

    for i in range(1, NC):
        push(cols.at[c], cols.at[c], "ag1", (t, mod(c + i, NC)))
    for i, (dt, dc) in enumerate(around):
        push(diff.at[4], diff.at[i if i < 4 else i + 1], "diff", (mod(t + dt, NT), mod(c + dc, NC)))
    for step in (SIDE, -SIDE):
        pl.semaphore_signal(hello, inc=1, device_id=(tile_at(step, k), c), device_id_type=MESH)
    loads[3].wait()
    usable = usable_in[...].astype(F32)
    usable = jnp.transpose(jnp.concatenate([usable] * 4, axis=0))
    for h in range(2):
        part = slice(h * 16, h * 16 + 16)
        seen = obs_send[part].astype(F32).reshape(TC, CH)
        seen = jnp.where(usable[:, h : h + 1] > 0.5, seen, UNUSED)
        obs_send[part] = seen.reshape(16, CAP, CH).astype(BF16)

    own_obs = pltpu.make_async_copy(obs_send.at[t], obs_recv.at[t], local.at[5])
    own_obs.start()

    def send_obs(peers):
        for dz, core in peers:
            to = tile_at(dz, core)
            push(obs_send.at[to], obs_recv.at[t], "obs", (to, c))

    send_obs(near)
    send_obs([(0, 1 - k)])
    for d in range(1, SIDE):
        to_x, to_y = mod(x + d, SIDE), mod(y + d, SIDE)
        push(gp.at[:, to_x, 0:HALF, :], r1a.at[d - 1], "r1a", (t, y * SIDE + to_x))
        push(gp.at[to_y, :, HALF:ROWS, :], r1b.at[d - 1], "r1b", (t, to_y * SIDE + x))
    pl.semaphore_wait(hello, 2)
    send_obs([(dz, core) for dz in (8, 7, -7, 6, -6, 5, -5) for core in (0, 1)])

    own_row = jnp.broadcast_to(owners_in[pl.ds(t, 1), :].astype(F32), (TC, TC))
    own_col = jnp.transpose(own_row)
    at_row = lax.broadcasted_iota(jnp.int32, (TC, TC), 0)
    at_lane = lax.broadcasted_iota(jnp.int32, (TC, TC), 1)
    earlier = jnp.where((own_row == own_col) & (at_lane < at_row), 1.0, 0.0)
    rank = jnp.sum(earlier, axis=1, keepdims=True)
    slot = (own_col[:, 0:1] * float(CAP) + rank).astype(jnp.int32)
    select = jnp.where(
        slot == lax.broadcasted_iota(jnp.int32, (TC, NT * CAP), 1), 1.0, 0.0
    ).astype(BF16)

    loads[4].wait()
    wait_recv("ag1")
    tile_cols = cols[...].astype(F32).reshape(TC, LANES)[:, 0:FEAT].astype(BF16)
    preact = jnp.dot(tile_cols, wh[...], preferred_element_type=F32) + bh_in[...]
    squash = jax.nn.sigmoid(preact)
    act[y, x] = (preact * squash).astype(BF16)
    slope = squash * (1.0 + preact * (1.0 - squash))
    gather("act")

    def add(own, got):
        acc = own.astype(F32)
        for d in range(SIDE - 1):
            acc = acc + got[d].astype(F32)
        return acc.astype(BF16)

    wait_recv("r1a")
    s1a[...] = add(gp[:, x, 0:HALF, :], r1a)
    wait_recv("r1b")
    s1b[...] = add(gp[y, :, HALF:ROWS, :], r1b)
    for d in range(1, SIDE):
        to_x, to_y = mod(x + d, SIDE), mod(y + d, SIDE)
        push(s1a.at[to_y], r2a.at[d - 1], "r2a", (t, to_y * SIDE + x))
        push(s1b.at[to_x], r2b.at[d - 1], "r2b", (t, y * SIDE + to_x))
    def block_of(at, core):
        return g_all.at[mod(z + at, NZ), core]

    def along(stage, i):
        at, by = STAGES[stage][i]
        block = block_of(at, k)
        return pltpu.make_async_remote_copy(
            src_ref=block, dst_ref=block, send_sem=ring_s.at[stage, i], recv_sem=ring_r.at[stage, i],
            device_id=(tile_at(by, k), c), device_id_type=MESH,
        )

    def across(stage, i, core):
        at, by = STAGES[stage][i] if stage < 3 else (0, 0)
        block = block_of(at - by, core)
        return pltpu.make_async_remote_copy(
            src_ref=block, dst_ref=block, send_sem=core_s.at[stage, i], recv_sem=core_r.at[stage, i],
            device_id=(z * 2 + 1 - k, c), device_id_type=MESH,
        )

    def stage_in(stage, only=None):
        for i in only or range(len(STAGES[stage])):
            along(stage, i).wait_recv()
            if stage < 2:
                got = STAGES[stage][i][0] - STAGES[stage][i][1]
                for j, (at, by) in enumerate(STAGES[stage + 1]):
                    if at == got:
                        along(stage + 1, j).start()
            across(stage, i, k).start()

    relay("act", 1, 3, 2)
    wait_recv("r2a")
    g_all[z, k, 0:HALF, :] = add(s1a[y], r2a)
    wait_recv("r2b")
    g_all[z, k, HALF:ROWS, :] = add(s1b[x], r2b)
    for i in range(len(STAGES[0])):
        along(0, i).start()
    across(3, 0, k).start()

    gathered("act")
    tile_act = jnp.concatenate([act[i // SIDE, i % SIDE] for i in range(NC)], axis=1)
    radiance = jnp.dot(tile_act, wr[...], preferred_element_type=F32)
    radiance = radiance + jnp.concatenate([br_in[i : i + 1, :] for i in range(3)], axis=1)
    own_obs.wait()
    wait_recv("obs")
    arrived = obs_recv[...].astype(F32).reshape(NT * CAP, CH).astype(BF16)
    seen = jnp.dot(select, arrived, preferred_element_type=F32)
    dep[y, x] = jnp.where(seen < UNUSED * 0.5, radiance - seen, 0.0).astype(BF16)
    gather("dep")
    stage_in(0, (0, 1))
    relay("dep", 1, 3, 2)
    stage_in(0, (2, 3))
    stage_in(1)

    wait_recv("diff")
    lane = lax.broadcasted_iota(jnp.int32, (8, 128), 1)
    row = lax.broadcasted_iota(jnp.int32, (8, 128), 0)
    bands = []
    for dc in range(3):
        west, mid, east = (diff[8 - (dt * 3 + dc)] for dt in range(3))
        bands.append(
            jnp.where(
                lane < 8,
                pltpu.roll(west, 104, 1),
                jnp.where(lane < 40, pltpu.roll(mid, 8, 1), pltpu.roll(east, 40, 1)),
            )
        )
    upper = jnp.where(c > 0, pltpu.roll(bands[0], 6, 0), 0.0)
    lower = jnp.where(c < NC - 1, pltpu.roll(bands[2], 6, 0), 0.0)
    root = jnp.where(row < 2, upper, jnp.where(row < 6, pltpu.roll(bands[1], 2, 0), lower))
    root = jnp.sqrt(jnp.where((lane < 6) | (lane > 41), 0.0, root))
    root = jnp.transpose(root)[0:48, :]
    to_east = root * pltpu.roll(root, 47, 0)
    to_west = root * pltpu.roll(root, 1, 0)

    gathered("dep")
    grad = jnp.zeros((TC, HID), F32)
    for stage in (3, 0, 1, 2):
        entries = STAGES[stage] if stage < 3 else ((0, 0),)
        if stage == 2:
            stage_in(2)
        for i, (at, by) in enumerate(entries):
            across(stage, i, 1 - k).wait_recv()
            block = mod(z + at - by, NZ)
            grad = grad + jnp.dot(
                dep[block // SIDE, lax.rem(block, SIDE)],
                g_all[block].reshape(2 * ROWS, HID),
                preferred_element_type=F32,
            )
    grad_pre = (grad * slope).astype(BF16)
    part = lax.dot_general(grad_pre, wh[...], (((1,), (1,)), ((), ())), preferred_element_type=F32)
    part = jnp.concatenate([part, jnp.zeros((TC, LANES - FEAT), F32)], axis=1)
    pgrad[...] = part.reshape(NC, OWN, LANES).astype(BF16)
    for i in range(1, NC):
        to = mod(c + i, NC)
        push(pgrad.at[to], rs5.at[i - 1], "rs5", (t, to))
    wait_recv("rs5")
    total = pgrad[c].astype(F32)
    for i in range(NC - 1):
        total = total + rs5[i].astype(F32)
    halo[4] = total * 0.0625
    for i, (dt, dc) in enumerate(around):
        push(halo.at[4], halo.at[i if i < 4 else i + 1], "halo", (mod(t + dt, NT), mod(c + dc, NC)))

    for name in SEMS:
        if name != "halo":
            wait_send(name)
    for stage, entries in enumerate(STAGES):
        for i in range(len(entries)):
            along(stage, i).wait_send()
            across(stage, i, k).wait_send()
    across(3, 0, k).wait_send()

    strips[...] = jnp.zeros((3, 48, LANES), F32)
    wait_recv("halo")
    for dc in range(3):
        west, mid, east = (halo[8 - (dt * 3 + dc)] for dt in range(3))
        strips[dc, 6:8, :] = jnp.broadcast_to(west[7:8, :], (2, LANES))
        strips[dc, 40:42, :] = jnp.broadcast_to(east[0:1, :], (2, LANES))
        for j in range(OWN):
            strips[dc, 8 + 4 * j : 12 + 4 * j, :] = jnp.broadcast_to(mid[j : j + 1, :], (4, LANES))
    wait_send("halo")

    def swept(mine, before, after, i):
        here = root[:, i : i + 1]
        shape = (48, LANES)
        wide = lambda v: jnp.broadcast_to(v, shape)
        value = mine + wide(here * root[:, i + 1 : i + 2]) * (after - mine)
        value = value + wide(here * root[:, i - 1 : i]) * (before - mine)
        value = value + wide(to_east[:, i : i + 1]) * (pltpu.roll(mine, 47, 0) - mine)
        return value + wide(to_west[:, i : i + 1]) * (pltpu.roll(mine, 1, 0) - mine)

    band = lambda i: strips[0 if i < 2 else (1 if i < 6 else 2)]
    for i in range(1, 7):
        sweep[i - 1] = swept(band(i), band(i - 1), band(i + 1), i)
    for i in range(2, 6):
        out[i - 2] = swept(sweep[i - 1], sweep[i - 2], sweep[i], i)[8:40, 0:FEAT]


def body(fields, diffusivity, owners, observed, usable, w_hidden, b_hidden, w_radiance, b_radiance, inv_cov):
    vmem, hbm = pl.BlockSpec(memory_space=pltpu.VMEM), pl.BlockSpec(memory_space=pl.ANY)
    n = len(SEMS)
    return pl.pallas_call(
        kernel,
        out_shape=jax.ShapeDtypeStruct((4, 32, FEAT), F32),
        in_specs=[hbm, vmem, vmem, hbm, vmem, hbm, vmem, hbm, vmem, hbm],
        out_specs=vmem,
        scratch_shapes=[
            pltpu.VMEM((4, 32, FEAT), F32),
            pltpu.VMEM((4, 32, 128), F32),
            pltpu.VMEM((NT, CAP, CH), BF16),
            pltpu.VMEM((NT, CAP, CH), BF16),
            pltpu.VMEM((FEAT, HID), BF16),
            pltpu.VMEM((ALL_HID, CH), BF16),
            pltpu.VMEM((ROWS, CH), BF16),
            pltpu.VMEM((NC, OWN, LANES), BF16),
            pltpu.VMEM((SIDE, SIDE, TC, HID), BF16),
            pltpu.VMEM((SIDE, SIDE, ROWS, HID), BF16),
            pltpu.VMEM((SIDE - 1, SIDE, HALF, HID), BF16),
            pltpu.VMEM((SIDE - 1, SIDE, HALF, HID), BF16),
            pltpu.VMEM((SIDE, HALF, HID), BF16),
            pltpu.VMEM((SIDE, HALF, HID), BF16),
            pltpu.VMEM((SIDE - 1, HALF, HID), BF16),
            pltpu.VMEM((SIDE - 1, HALF, HID), BF16),
            pltpu.VMEM((NZ, 2, ROWS, HID), BF16),
            pltpu.VMEM((SIDE, SIDE, TC, CH), BF16),
            pltpu.VMEM((NC, OWN, LANES), BF16),
            pltpu.VMEM((NC - 1, OWN, LANES), BF16),
            pltpu.VMEM((9, OWN, LANES), F32),
            pltpu.VMEM((9, 8, 128), F32),
            pltpu.VMEM((3, 48, LANES), F32),
            pltpu.VMEM((6, 48, LANES), F32),
            pltpu.SemaphoreType.DMA((6,)),
            pltpu.SemaphoreType.DMA((n,)),
            pltpu.SemaphoreType.DMA((n,)),
            pltpu.SemaphoreType.DMA((3, 6)),
            pltpu.SemaphoreType.DMA((3, 6)),
            pltpu.SemaphoreType.DMA((4, 6)),
            pltpu.SemaphoreType.DMA((4, 6)),
            pltpu.SemaphoreType.REGULAR,
        ],
        compiler_params=pltpu.CompilerParams(collective_id=0, has_side_effects=True),
    )(
        fields,
        diffusivity,
        owners.reshape(NT, TC),
        observed.reshape(NT, CAP, CH),
        usable.reshape(2, 128),
        w_hidden,
        b_hidden.reshape(1, HID),
        w_radiance,
        b_radiance.reshape(3, 128),
        inv_cov,
    )


def solution(mesh):
    placed = (
        P("chan", "tile", None), P("chan", "tile"), P(), P("tile", "chan"), P("tile"),
        P(None, "chan"), P("chan"), P(None, "chan"), P("chan"), P("tile", "chan"),
    )
    return jax.shard_map(
        body, mesh=mesh, in_specs=placed, out_specs=P("chan", "tile", None), check_vma=False
    )
```

```python
import jax
import jax.numpy as jnp
from jax import lax
from jax.experimental import pallas as pl
from jax.experimental.pallas import tpu as pltpu
from jax.sharding import PartitionSpec as P

MESH = pl.DeviceIdType.MESH
F32, BF16 = jnp.float32, jnp.bfloat16
NZ, SIDE, NC, NT = 16, 4, 16, 32
CAP = 8
OWN = 8
TC = 128
FEAT, LANES = 411, 512
HID, ALL_HID = 128, 2048
CH = 384
ROWS = 192
HALF = ROWS // 2
UNUSED = 2.0**100

SEMS = (
    "ag1", "diff", "obs", "r1a", "r1b", "r2a", "r2b", "rs5", "halo",
    *(who + part for who in ("act", "dep") for part in ("x1", "x2", "x3", "y1", "y2", "y3", "over_y", "over_x")),
)
STAGES = (
    ((0, 3), (0, -3), (0, 1), (0, -1)),
    ((-3, 3), (3, -3), (-3, 1), (3, -1), (-3, -1), (3, 1)),
    ((-6, 2), (-6, 1), (6, -1), (-6, -1), (6, 1)),
)


def kernel(
    fields_h, diff_in, owners_in, obs_h, usable_in, wh_h, bh_in, wr_h, br_in, ic_h,
    out,
    fields, quads, obs_send, obs_recv, wh, wr, ic,
    cols, act, gp, r1a, r1b, s1a, s1b, r2a, r2b, g_all, dep, pgrad, rs5, halo, diff, strips, sweep,
    local, send, recv, ring_s, ring_r, core_s, core_r, hello,
):
    t, c = lax.axis_index("tile"), lax.axis_index("chan")
    z, k = t // 2, t % 2
    y, x = c // SIDE, c % SIDE
    sem_of = {name: i for i, name in enumerate(SEMS)}

    def tile_at(dz, core):
        return lax.rem(z + dz + NZ, NZ) * 2 + core

    def mod(v, n):
        return lax.rem(v + n, n)

    def push(src, dst, name, where):
        i = sem_of[name]
        pltpu.make_async_remote_copy(
            src_ref=src, dst_ref=dst, send_sem=send.at[i], recv_sem=recv.at[i],
            device_id=where, device_id_type=MESH,
        ).start()

    lo, hi = slice(0, TC // 2), slice(TC // 2, TC)
    whole = {
        "ag1": cols.at[0 : NC - 1], "diff": diff.at[0:8], "obs": obs_recv.at[0 : NT - 1],
        "r1a": r1a, "r1b": r1b, "r2a": r2a, "r2b": r2b, "rs5": rs5, "halo": halo.at[0:8],
    }
    blocks_of = {"act": act, "dep": dep}
    for who, buf in blocks_of.items():
        for d in range(1, SIDE):
            whole[f"{who}x{d}"] = buf.at[0, 0, lo, :]
            whole[f"{who}y{d}"] = buf.at[0, 0, hi, :]
        whole[who + "over_y"] = buf.at[0:3, :, lo, :]
        whole[who + "over_x"] = buf.at[0:3, :, hi, :]

    def wait_recv(name):
        pltpu.make_async_copy(whole[name], whole[name], recv.at[sem_of[name]]).wait()

    def wait_send(name):
        pltpu.make_async_copy(whole[name], whole[name], send.at[sem_of[name]]).wait()

    def over_y(who, xx):
        block = blocks_of[who].at[y, xx, lo, :]
        for d in (2, 1, 3):
            push(block, block, who + "over_y", (t, mod(y + d, SIDE) * SIDE + x))

    def over_x(who, yy):
        block = blocks_of[who].at[yy, x, hi, :]
        for d in (2, 1, 3):
            push(block, block, who + "over_x", (t, y * SIDE + mod(x + d, SIDE)))

    def gather(who):
        upper, lower = blocks_of[who].at[y, x, lo, :], blocks_of[who].at[y, x, hi, :]
        for d in (2, 1, 3):
            push(upper, upper, f"{who}x{d}", (t, y * SIDE + mod(x + d, SIDE)))
            push(lower, lower, f"{who}y{d}", (t, mod(y + d, SIDE) * SIDE + x))
        over_y(who, x)
        over_x(who, y)

    def relay(who, *steps):
        for d in steps:
            wait_recv(f"{who}x{d}")
            over_y(who, mod(x - d, SIDE))
            wait_recv(f"{who}y{d}")
            over_x(who, mod(y - d, SIDE))

    def gathered(who):
        wait_recv(who + "over_y")
        wait_recv(who + "over_x")

    loads = [
        pltpu.make_async_copy(src, dst, local.at[i])
        for i, (src, dst) in enumerate(
            [(fields_h, fields), (ic_h, ic), (wr_h, wr), (obs_h, obs_send), (wh_h, wh)]
        )
    ]
    for copy in loads:
        copy.start()
    near = [(dz, core) for dz in (4, -4, 3, -3, 2, -2, 1, -1) for core in (0, 1)]
    around = [(dt, dc) for dt in (-1, 0, 1) for dc in (-1, 0, 1) if (dt, dc) != (0, 0)]
    barrier = pltpu.get_barrier_semaphore()
    greeted = [(t, mod(c + i, NC)) for i in range(1, NC)]
    greeted += [(tile_at(dz, core), c) for dz, core in near] + [(z * 2 + 1 - k, c)]
    greeted += [(mod(t + dt, NT), mod(c + dc, NC)) for dt, dc in around if dt and dc]
    for where in greeted:
        pl.semaphore_signal(barrier, inc=1, device_id=where, device_id_type=MESH)

    loads[0].wait()
    summed = fields[0] + fields[1] + fields[2] + fields[3]
    for b in range(LANES // 128):
        width = min(128, FEAT - b * 128)
        quads[b] = jnp.zeros((32, 128), F32)
        quads[b, :, 0:width] = summed[:, b * 128 : b * 128 + width]
        total = None
        for j in range(4):
            part = quads[b, pl.ds(j, OWN, stride=4), :]
            total = part if total is None else total + part
        cols[c, :, b * 128 : b * 128 + 128] = (total * 0.0625).astype(BF16)

    diff[4] = jnp.zeros((8, 128), F32)
    diff[4, 0:4, 0:32] = diff_in[...]

    loads[1].wait()
    loads[2].wait()
    cov = ic[...]
    for b in range(NC // 2):
        part = lax.dot_general(
            cov, wr[b * 256 : b * 256 + 256, :], (((1,), (1,)), ((), ())), preferred_element_type=F32
        ).astype(BF16)
        for h in range(2):
            q = 2 * b + h
            gp[q // SIDE, q % SIDE] = part[:, h * 128 : h * 128 + 128]

    pl.semaphore_wait(barrier, len(greeted))

    for i in range(1, NC):
        push(cols.at[c], cols.at[c], "ag1", (t, mod(c + i, NC)))
    for d in range(1, SIDE):
        to_x, to_y = mod(x + d, SIDE), mod(y + d, SIDE)
        push(gp.at[:, to_x, 0:HALF, :], r1a.at[d - 1], "r1a", (t, y * SIDE + to_x))
        push(gp.at[to_y, :, HALF:ROWS, :], r1b.at[d - 1], "r1b", (t, to_y * SIDE + x))
    for i, (dt, dc) in enumerate(around):
        push(diff.at[4], diff.at[i if i < 4 else i + 1], "diff", (mod(t + dt, NT), mod(c + dc, NC)))
    for step in (SIDE, -SIDE):
        pl.semaphore_signal(hello, inc=1, device_id=(tile_at(step, k), c), device_id_type=MESH)
    loads[3].wait()
    usable = usable_in[...].astype(F32)
    usable = jnp.transpose(jnp.concatenate([usable] * 4, axis=0))
    for h in range(2):
        part = slice(h * 16, h * 16 + 16)
        seen = obs_send[part].astype(F32).reshape(TC, CH)
        seen = jnp.where(usable[:, h : h + 1] > 0.5, seen, UNUSED)
        obs_send[part] = seen.reshape(16, CAP, CH).astype(BF16)

    own_obs = pltpu.make_async_copy(obs_send.at[t], obs_recv.at[t], local.at[5])
    own_obs.start()

    def send_obs(peers):
        for dz, core in peers:
            to = tile_at(dz, core)
            push(obs_send.at[to], obs_recv.at[t], "obs", (to, c))

    send_obs(near)
    send_obs([(0, 1 - k)])
    pl.semaphore_wait(hello, 2)
    send_obs([(dz, core) for dz in (8, 7, -7, 6, -6, 5, -5) for core in (0, 1)])

    own_row = jnp.broadcast_to(owners_in[pl.ds(t, 1), :].astype(F32), (TC, TC))
    own_col = jnp.transpose(own_row)
    at_row = lax.broadcasted_iota(jnp.int32, (TC, TC), 0)
    at_lane = lax.broadcasted_iota(jnp.int32, (TC, TC), 1)
    earlier = jnp.where((own_row == own_col) & (at_lane < at_row), 1.0, 0.0)
    rank = jnp.sum(earlier, axis=1, keepdims=True)
    slot = (own_col[:, 0:1] * float(CAP) + rank).astype(jnp.int32)
    select = jnp.where(
        slot == lax.broadcasted_iota(jnp.int32, (TC, NT * CAP), 1), 1.0, 0.0
    ).astype(BF16)

    loads[4].wait()
    wait_recv("ag1")
    tile_cols = cols[...].astype(F32).reshape(TC, LANES)[:, 0:FEAT].astype(BF16)
    preact = jnp.dot(tile_cols, wh[...], preferred_element_type=F32) + bh_in[...]
    squash = jax.nn.sigmoid(preact)
    act[y, x] = (preact * squash).astype(BF16)
    slope = squash * (1.0 + preact * (1.0 - squash))
    gather("act")

    def add(own, got):
        acc = own.astype(F32)
        for d in range(SIDE - 1):
            acc = acc + got[d].astype(F32)
        return acc.astype(BF16)

    wait_recv("r1a")
    s1a[...] = add(gp[:, x, 0:HALF, :], r1a)
    wait_recv("r1b")
    s1b[...] = add(gp[y, :, HALF:ROWS, :], r1b)
    for d in range(1, SIDE):
        to_x, to_y = mod(x + d, SIDE), mod(y + d, SIDE)
        push(s1a.at[to_y], r2a.at[d - 1], "r2a", (t, to_y * SIDE + x))
        push(s1b.at[to_x], r2b.at[d - 1], "r2b", (t, y * SIDE + to_x))
    def block_of(at, core):
        return g_all.at[mod(z + at, NZ), core]

    def along(stage, i):
        at, by = STAGES[stage][i]
        block = block_of(at, k)
        return pltpu.make_async_remote_copy(
            src_ref=block, dst_ref=block, send_sem=ring_s.at[stage, i], recv_sem=ring_r.at[stage, i],
            device_id=(tile_at(by, k), c), device_id_type=MESH,
        )

    def across(stage, i, core):
        at, by = STAGES[stage][i] if stage < 3 else (0, 0)
        block = block_of(at - by, core)
        return pltpu.make_async_remote_copy(
            src_ref=block, dst_ref=block, send_sem=core_s.at[stage, i], recv_sem=core_r.at[stage, i],
            device_id=(z * 2 + 1 - k, c), device_id_type=MESH,
        )

    def stage_in(stage, only=None):
        for i in only or range(len(STAGES[stage])):
            along(stage, i).wait_recv()
            if stage < 2:
                got = STAGES[stage][i][0] - STAGES[stage][i][1]
                for j, (at, by) in enumerate(STAGES[stage + 1]):
                    if at == got:
                        along(stage + 1, j).start()
            across(stage, i, k).start()

    relay("act", 1, 3, 2)
    wait_recv("r2a")
    g_all[z, k, 0:HALF, :] = add(s1a[y], r2a)
    wait_recv("r2b")
    g_all[z, k, HALF:ROWS, :] = add(s1b[x], r2b)
    for i in range(len(STAGES[0])):
        along(0, i).start()
    across(3, 0, k).start()

    gathered("act")
    tile_act = jnp.concatenate([act[i // SIDE, i % SIDE] for i in range(NC)], axis=1)
    radiance = jnp.dot(tile_act, wr[...], preferred_element_type=F32)
    radiance = radiance + jnp.concatenate([br_in[i : i + 1, :] for i in range(3)], axis=1)
    own_obs.wait()
    wait_recv("obs")
    arrived = obs_recv[...].astype(F32).reshape(NT * CAP, CH).astype(BF16)
    seen = jnp.dot(select, arrived, preferred_element_type=F32)
    dep[y, x] = jnp.where(seen < UNUSED * 0.5, radiance - seen, 0.0).astype(BF16)
    gather("dep")
    stage_in(0, (0, 1))
    relay("dep", 1, 3, 2)
    stage_in(0, (2, 3))
    stage_in(1)

    wait_recv("diff")
    lane = lax.broadcasted_iota(jnp.int32, (8, 128), 1)
    row = lax.broadcasted_iota(jnp.int32, (8, 128), 0)
    bands = []
    for dc in range(3):
        west, mid, east = (diff[8 - (dt * 3 + dc)] for dt in range(3))
        bands.append(
            jnp.where(
                lane < 8,
                pltpu.roll(west, 104, 1),
                jnp.where(lane < 40, pltpu.roll(mid, 8, 1), pltpu.roll(east, 40, 1)),
            )
        )
    upper = jnp.where(c > 0, pltpu.roll(bands[0], 6, 0), 0.0)
    lower = jnp.where(c < NC - 1, pltpu.roll(bands[2], 6, 0), 0.0)
    root = jnp.where(row < 2, upper, jnp.where(row < 6, pltpu.roll(bands[1], 2, 0), lower))
    root = jnp.sqrt(jnp.where((lane < 6) | (lane > 41), 0.0, root))
    root = jnp.transpose(root)[0:48, :]
    to_east = root * pltpu.roll(root, 47, 0)
    to_west = root * pltpu.roll(root, 1, 0)

    gathered("dep")
    grad = jnp.zeros((TC, HID), F32)
    for stage in (3, 0, 1, 2):
        entries = STAGES[stage] if stage < 3 else ((0, 0),)
        if stage == 2:
            stage_in(2)
        for i, (at, by) in enumerate(entries):
            across(stage, i, 1 - k).wait_recv()
            block = mod(z + at - by, NZ)
            grad = grad + jnp.dot(
                dep[block // SIDE, lax.rem(block, SIDE)],
                g_all[block].reshape(2 * ROWS, HID),
                preferred_element_type=F32,
            )
    grad_pre = (grad * slope).astype(BF16)
    part = lax.dot_general(grad_pre, wh[...], (((1,), (1,)), ((), ())), preferred_element_type=F32)
    part = jnp.concatenate([part, jnp.zeros((TC, LANES - FEAT), F32)], axis=1)
    pgrad[...] = part.reshape(NC, OWN, LANES).astype(BF16)
    for i in range(1, NC):
        to = mod(c + i, NC)
        push(pgrad.at[to], rs5.at[i - 1], "rs5", (t, to))
    wait_recv("rs5")
    total = pgrad[c].astype(F32)
    for i in range(NC - 1):
        total = total + rs5[i].astype(F32)
    halo[4] = total * 0.0625
    for i, (dt, dc) in enumerate(around):
        push(halo.at[4], halo.at[i if i < 4 else i + 1], "halo", (mod(t + dt, NT), mod(c + dc, NC)))

    for name in SEMS:
        if name != "halo":
            wait_send(name)
    for stage, entries in enumerate(STAGES):
        for i in range(len(entries)):
            along(stage, i).wait_send()
            across(stage, i, k).wait_send()
    across(3, 0, k).wait_send()

    strips[...] = jnp.zeros((3, 48, LANES), F32)
    wait_recv("halo")
    for dc in range(3):
        west, mid, east = (halo[8 - (dt * 3 + dc)] for dt in range(3))
        strips[dc, 6:8, :] = jnp.broadcast_to(west[7:8, :], (2, LANES))
        strips[dc, 40:42, :] = jnp.broadcast_to(east[0:1, :], (2, LANES))
        for j in range(OWN):
            strips[dc, 8 + 4 * j : 12 + 4 * j, :] = jnp.broadcast_to(mid[j : j + 1, :], (4, LANES))
    wait_send("halo")

    def swept(mine, before, after, i):
        here = root[:, i : i + 1]
        shape = (48, LANES)
        wide = lambda v: jnp.broadcast_to(v, shape)
        value = mine + wide(here * root[:, i + 1 : i + 2]) * (after - mine)
        value = value + wide(here * root[:, i - 1 : i]) * (before - mine)
        value = value + wide(to_east[:, i : i + 1]) * (pltpu.roll(mine, 47, 0) - mine)
        return value + wide(to_west[:, i : i + 1]) * (pltpu.roll(mine, 1, 0) - mine)

    band = lambda i: strips[0 if i < 2 else (1 if i < 6 else 2)]
    for i in range(1, 7):
        sweep[i - 1] = swept(band(i), band(i - 1), band(i + 1), i)
    for i in range(2, 6):
        out[i - 2] = swept(sweep[i - 1], sweep[i - 2], sweep[i], i)[8:40, 0:FEAT]


def body(fields, diffusivity, owners, observed, usable, w_hidden, b_hidden, w_radiance, b_radiance, inv_cov):
    vmem, hbm = pl.BlockSpec(memory_space=pltpu.VMEM), pl.BlockSpec(memory_space=pl.ANY)
    n = len(SEMS)
    return pl.pallas_call(
        kernel,
        out_shape=jax.ShapeDtypeStruct((4, 32, FEAT), F32),
        in_specs=[hbm, vmem, vmem, hbm, vmem, hbm, vmem, hbm, vmem, hbm],
        out_specs=vmem,
        scratch_shapes=[
            pltpu.VMEM((4, 32, FEAT), F32),
            pltpu.VMEM((4, 32, 128), F32),
            pltpu.VMEM((NT, CAP, CH), BF16),
            pltpu.VMEM((NT, CAP, CH), BF16),
            pltpu.VMEM((FEAT, HID), BF16),
            pltpu.VMEM((ALL_HID, CH), BF16),
            pltpu.VMEM((ROWS, CH), BF16),
            pltpu.VMEM((NC, OWN, LANES), BF16),
            pltpu.VMEM((SIDE, SIDE, TC, HID), BF16),
            pltpu.VMEM((SIDE, SIDE, ROWS, HID), BF16),
            pltpu.VMEM((SIDE - 1, SIDE, HALF, HID), BF16),
            pltpu.VMEM((SIDE - 1, SIDE, HALF, HID), BF16),
            pltpu.VMEM((SIDE, HALF, HID), BF16),
            pltpu.VMEM((SIDE, HALF, HID), BF16),
            pltpu.VMEM((SIDE - 1, HALF, HID), BF16),
            pltpu.VMEM((SIDE - 1, HALF, HID), BF16),
            pltpu.VMEM((NZ, 2, ROWS, HID), BF16),
            pltpu.VMEM((SIDE, SIDE, TC, CH), BF16),
            pltpu.VMEM((NC, OWN, LANES), BF16),
            pltpu.VMEM((NC - 1, OWN, LANES), BF16),
            pltpu.VMEM((9, OWN, LANES), F32),
            pltpu.VMEM((9, 8, 128), F32),
            pltpu.VMEM((3, 48, LANES), F32),
            pltpu.VMEM((6, 48, LANES), F32),
            pltpu.SemaphoreType.DMA((6,)),
            pltpu.SemaphoreType.DMA((n,)),
            pltpu.SemaphoreType.DMA((n,)),
            pltpu.SemaphoreType.DMA((3, 6)),
            pltpu.SemaphoreType.DMA((3, 6)),
            pltpu.SemaphoreType.DMA((4, 6)),
            pltpu.SemaphoreType.DMA((4, 6)),
            pltpu.SemaphoreType.REGULAR,
        ],
        compiler_params=pltpu.CompilerParams(collective_id=0, has_side_effects=True),
    )(
        fields,
        diffusivity,
        owners.reshape(NT, TC),
        observed.reshape(NT, CAP, CH),
        usable.reshape(2, 128),
        w_hidden,
        b_hidden.reshape(1, HID),
        w_radiance,
        b_radiance.reshape(3, 128),
        inv_cov,
    )


def solution(mesh):
    placed = (
        P("chan", "tile", None), P("chan", "tile"), P(), P("tile", "chan"), P("tile"),
        P(None, "chan"), P("chan"), P(None, "chan"), P("chan"), P("tile", "chan"),
    )
    return jax.shard_map(
        body, mesh=mesh, in_specs=placed, out_specs=P("chan", "tile", None), check_vma=False
    )
```
